128 devices in a mesh: layer: 2 (over core), latent: 64 (over y, x, z).
Axes of the slice: x: 4, y: 4, z: 4, core: 2. Of those that a mesh axis runs over, the one named last changes fastest.
Arguments:
- activations: bfloat16 [2, 512, 2048], P('layer', 'latent'), may hold values from -15 to 15
- enc_weight: bfloat16 [2, 2048, 65536], P('layer', None, 'latent'), may hold values from -0.09375 to 0.09375
- enc_bias: float32 [65536], P('latent'), may hold values from -3 to 3
- dec_weight: bfloat16 [2, 65536, 2048], P('layer', 'latent'), may hold values from -0.08984375 to 0.08984375
- dec_bias: float32 [2, 2048], P('layer'), may hold values from -3 to 3
- active_mask: int32 [512, 65536], P(None, 'latent'), may hold values 0 or 1
Outputs:
- grad_enc: bfloat16 [2, 2048, 65536], P('layer', None, 'latent')
- grad_dec: bfloat16 [2, 65536, 2048], P('layer', 'latent')
- loss_value: float32 [], replicated
The draws below stay inside these ranges and needn't reach their ends.
All inputs are finite; a program needn't handle non-finite values. No bound on the sum of `active_mask` on one device may be relied on, other than what follows from the above.
Results may differ from the reference program's by a relative error of at most 0.0065.
Values may be sent and summed in bfloat16 or wider, within the bound.
No kernel may reach another device: no remote copies, remote signals or barrier semaphores. Data moves between devices by JAX's collectives and lax.ppermute only.
A program may use at most 128 MiB of HBM per device.

```python
import jax
import jax.numpy as jnp
from jax import lax

D = 2048
TOK = 512
LAYERS = 2
LATENTS = 65536


def draw_activations(key, part):
    first = jax.random.fold_in(key, 0)
    layer_scale = 1.0 + 0.8 * jnp.arange(LAYERS, dtype=jnp.float32)[:, None, None] / max(LAYERS - 1, 1)
    base = jnp.clip(jax.random.normal(first, (LAYERS, TOK, D), jnp.float32), -7.0, 7.0)
    values = base * layer_scale
    return values.astype(jnp.bfloat16)


def draw_dec_weight(key, part):
    first = jax.random.fold_in(key, 0)
    rising = 3.0 ** (jnp.arange(LATENTS, dtype=jnp.float32) / LATENTS)
    layer_scale = 1.0 + 0.8 * jnp.arange(LAYERS, dtype=jnp.float32)[:, None, None] / max(LAYERS - 1, 1)
    factor = (2.0 * LATENTS) ** (-0.5)
    base = jnp.clip(jax.random.normal(first, (LAYERS, LATENTS, D), jnp.float32), -6.0, 6.0)
    values = base * rising[None, :, None] * layer_scale * factor
    return values.astype(jnp.bfloat16)


def touch_ends(array, stream_key, smallest, top_value):
    dims = array.shape
    place = [jax.random.randint(jax.random.fold_in(stream_key, axis), (), 0, dims[axis]) for axis in range(len(dims))]
    array = array.at[tuple(place)].set(smallest)
    longest = dims.index(max(dims))
    place[longest] = (place[longest] + 1) % dims[longest]
    return array.at[tuple(place)].set(top_value)


def block_scale(key, dims, shards, least, largest):
    factor_of = 1.0
    for position, blocks in shards:
        heights = jax.random.uniform(jax.random.fold_in(jax.random.fold_in(key, 6), position), (blocks,), jnp.float32, least / len(shards), largest / len(shards))
        factor_of = factor_of * jnp.repeat(jnp.exp(heights), dims[position] // blocks).reshape((-1,) + (1,) * (len(dims) - 1 - position))
    return factor_of


def scatter_about(rng, shape, width, limit, cuts=(), kind=jnp.bfloat16):
    drawn = jax.random.normal(rng, shape, jnp.float32) * width
    if len(cuts) > 0:
        drawn = block_scale(rng, shape, cuts, -0.22, 0.18) * drawn
    return jnp.clip(drawn, min=-limit, max=limit).astype(kind)


def setup_inputs(seed: int = 0) -> dict:
    streams_of = jax.random.split(jax.random.key(seed), 7)
    return {
        "activations": draw_activations(jax.random.fold_in(streams_of[6], 71), 0),
        "enc_weight": scatter_about(streams_of[1], (LAYERS, D, LATENTS), (LAYERS * D) ** -0.5, 0.09375, ((0, 2), (2, 64))),
        "enc_bias": scatter_about(streams_of[2], (LATENTS,), 0.5, 3.0, ((0, 64),), jnp.float32),
        "dec_weight": draw_dec_weight(jax.random.fold_in(streams_of[6], 71), 0),
        "dec_bias": scatter_about(streams_of[4], (LAYERS, D), 0.5, 3.0, ((0, 2),), jnp.float32),
        "active_mask": touch_ends((jax.random.randint(streams_of[5], (TOK, LATENTS), 0, 4) < 1).astype(jnp.int32), jax.random.fold_in(streams_of[5], 1), 0, 1),
    }


sparsity_weight = 0.4

def reference(activations, enc_weight, enc_bias, dec_weight, dec_bias, active_mask):
    preact = jnp.zeros((TOK, LATENTS), jnp.float32)
    for layer in range(LAYERS):
        preact = preact + jnp.dot(activations[layer], enc_weight[layer], preferred_element_type=jnp.float32)
    preact = preact + enc_bias
    gating = active_mask.astype(jnp.float32)
    latent_code = preact * gating
    code_b = latent_code.astype(jnp.bfloat16)
    norm_list = []
    for layer in range(LAYERS):
        dec_float = dec_weight[layer].astype(jnp.float32)
        norm_list.append(jnp.sqrt(lax.optimization_barrier(jnp.sum(dec_float * dec_float, axis=1)) + 1e-06))
    norm_sum = norm_list[0]
    for layer in range(1, LAYERS):
        norm_sum = norm_sum + norm_list[layer]
    square_part = jnp.float32(0.0)
    error_list = []
    code_grad = jnp.zeros((TOK, LATENTS), jnp.float32)
    for layer in range(LAYERS):
        recon = jnp.dot(code_b, dec_weight[layer], preferred_element_type=jnp.float32) + dec_bias[layer]
        error_full = recon - activations[layer].astype(jnp.float32)
        square_part = square_part + 0.5 * jnp.sum(error_full * error_full)
        error_b = error_full.astype(jnp.bfloat16)
        error_list.append(error_b)
        code_grad = code_grad + jnp.dot(error_b, dec_weight[layer].T, preferred_element_type=jnp.float32)
    code_grad = code_grad + sparsity_weight * norm_sum
    preact_grad = (code_grad * gating).astype(jnp.bfloat16)
    code_total = lax.optimization_barrier(jnp.sum(latent_code, axis=0))
    enc_list = []
    dec_list = []
    for layer in range(LAYERS):
        enc_list.append(jnp.dot(activations[layer].T, preact_grad, preferred_element_type=jnp.float32).astype(jnp.bfloat16))
        dec_float = dec_weight[layer].astype(jnp.float32)
        shrink = sparsity_weight * code_total[:, None] * dec_float / norm_list[layer][:, None]
        dec_list.append((jnp.dot(code_b.T, error_list[layer], preferred_element_type=jnp.float32) + shrink).astype(jnp.bfloat16))
    sparse_part = sparsity_weight * jnp.sum(latent_code * norm_sum)
    loss_value = (square_part + sparse_part) / (TOK * D)
    return (jnp.stack(enc_list), jnp.stack(dec_list), loss_value)
```

```python
import functools

import jax
import jax.numpy as jnp
from jax import lax
from jax.experimental import pallas as pl
from jax.experimental.pallas import tpu as pltpu
from jax.sharding import Mesh
from jax.sharding import PartitionSpec as P

LATENT = ("latent_0", "latent_1", "latent_2")
SPARSITY = 0.4
EXTRA = 128
MIB = 1 << 20


def swap_layers(x):
    return lax.ppermute(x, "layer", [(0, 1), (1, 0)])


def send_to_all(x):
    count = lax.axis_size(LATENT)
    return lax.all_to_all(jnp.broadcast_to(x[None], (count, *x.shape)), LATENT, 0, 0, tiled=True)


def split_float(x):
    high = lax.reduce_precision(x, 8, 7)
    middle = lax.reduce_precision(x - high, 8, 7)
    low = lax.reduce_precision(x - high - middle, 8, 7)
    return high, middle, low


def outer_kernel(a_ref, b_ref, o_ref):
    o_ref[...] = lax.dot_general(
        a_ref[...], b_ref[...], (((0,), (0,)), ((), ())), preferred_element_type=jnp.float32
    ).astype(o_ref.dtype)


def grad_encoder(tokens, preact_grad, block=256):
    count, features = tokens.shape
    latents = preact_grad.shape[1]
    return pl.pallas_call(
        outer_kernel,
        out_shape=jax.ShapeDtypeStruct((features, latents), jnp.bfloat16),
        grid=(features // block,),
        in_specs=[
            pl.BlockSpec((count, block), lambda i: (0, i)),
            pl.BlockSpec((count, latents), lambda i: (0, 0)),
        ],
        out_specs=pl.BlockSpec((block, latents), lambda i: (i, 0)),
        compiler_params=pltpu.CompilerParams(vmem_limit_bytes=32 * MIB),
    )(tokens, preact_grad)


def per_device(activations, enc_weight, enc_bias, dec_weight, dec_bias, active_mask):
    rows = activations[0]
    encoder = enc_weight[0]
    decoder = dec_weight[0]
    own, features = rows.shape
    tokens, latents = active_mask.shape
    token_all = send_to_all(rows).reshape(tokens, features)
    layer_pre = jnp.dot(token_all, encoder, preferred_element_type=jnp.float32)
    preact = layer_pre + swap_layers(layer_pre) + enc_bias
    dec_float = decoder.astype(jnp.float32)
    row_norm = jnp.sqrt(jnp.sum(dec_float * dec_float, axis=1) + 1e-06)
    gating = active_mask.astype(jnp.float32)
    latent_code = preact * gating
    code_b = latent_code.astype(jnp.bfloat16)
    code_total = jnp.sum(latent_code, axis=0)
    partial = jnp.dot(code_b, decoder, preferred_element_type=jnp.float32).astype(jnp.bfloat16)
    parts = lax.all_to_all(partial.reshape(-1, own, features), LATENT, 0, 0, tiled=True)
    error = jnp.sum(parts.astype(jnp.float32), axis=0) + dec_bias - rows.astype(jnp.float32)
    loss_part = 0.5 * jnp.sum(error * error) + SPARSITY * jnp.sum(code_total * row_norm)
    terms = jnp.stack(split_float(loss_part))
    extra = jnp.zeros((own, EXTRA), jnp.float32).at[0, :3].set(terms)
    sent = jnp.concatenate([error, extra], axis=1).astype(jnp.bfloat16)
    got = send_to_all(sent)
    error_b = got[:, :, :features].reshape(tokens, features)
    layer_loss = jnp.sum(got[:, 0, features : features + 3].astype(jnp.float32))
    layer_grad = jnp.einsum("td,fd->tf", error_b, decoder, preferred_element_type=jnp.float32)
    layer_grad = layer_grad + SPARSITY * row_norm
    code_grad = layer_grad + swap_layers(layer_grad)
    loss_value = (layer_loss + swap_layers(layer_loss)) / (tokens * features)
    preact_grad = (code_grad * gating).astype(jnp.bfloat16)
    grad_enc = grad_encoder(token_all, preact_grad)
    shrink = SPARSITY * code_total[:, None] * dec_float / row_norm[:, None]
    grad_dec = (
        jnp.einsum("tf,td->fd", code_b, error_b, preferred_element_type=jnp.float32) + shrink
    ).astype(jnp.bfloat16)
    return (grad_enc[None], grad_dec[None], loss_value)


def solution(mesh):
    torus = Mesh(
        mesh.devices.reshape(mesh.shape["layer"], 4, 4, 4),
        ("layer", *LATENT),
    )
    placed = (
        P("layer", LATENT, None),
        P("layer", None, LATENT),
        P(LATENT),
        P("layer", LATENT, None),
        P("layer", None),
        P(None, LATENT),
    )
    return jax.shard_map(
        per_device,
        mesh=torus,
        in_specs=placed,
        out_specs=(P("layer", None, LATENT), P("layer", LATENT, None), P()),
        check_vma=False,
    )
```

```python
import functools

import jax
import jax.numpy as jnp
from jax import lax
from jax.experimental import pallas as pl
from jax.experimental.pallas import tpu as pltpu
from jax.sharding import Mesh
from jax.sharding import PartitionSpec as P

LATENT = ("latent_0", "latent_1", "latent_2")
SIDE = 4
CHIPS = SIDE**3
SPARSITY = 0.4
EXTRA = 128
MIB = 1 << 20
F32 = jnp.float32
BF16 = jnp.bfloat16

STEPS = ((0, 1), (1, 0), (0, -1))


def class_groups():
    groups = [[] for _ in range(SIDE)]
    for chip in range(CHIPS):
        l0, l1 = chip // 16, chip // 4 % 4
        groups[(l1 + 2 * l0) % SIDE].append(chip)
    return groups


def moved(step, sign):
    pairs = []
    for chip in range(CHIPS):
        l0, l1, l2 = chip // 16, chip // 4 % 4, chip % 4
        target = (l0 + sign * step[0]) % 4 * 16 + (l1 + sign * step[1]) % 4 * 4 + l2
        pairs.append((chip, target))
    return pairs


def class_exchange(x):
    return lax.all_to_all(x, LATENT, 0, 0, axis_index_groups=class_groups(), tiled=True)


def from_neighbours(x):
    return [lax.ppermute(x, LATENT, moved(step, -1)) for step in STEPS]


def to_neighbours(parts):
    return [lax.ppermute(x, LATENT, moved(step, 1)) for x, step in zip(parts, STEPS)]


def swap_layers(x):
    return lax.ppermute(x, "layer", [(0, 1), (1, 0)])


def params(mib=40):
    return pltpu.CompilerParams(vmem_limit_bytes=mib * MIB)


def cost(flops, *arrays):
    size = sum(a.size * a.dtype.itemsize for a in arrays)
    return pl.CostEstimate(flops=flops, bytes_accessed=size, transcendentals=0)


def whole(shape):
    return pl.BlockSpec(shape, lambda *_: (0,) * len(shape))


def gate_kernel(class_ref, mask_ref, gate_ref):
    gate_ref[...] = mask_ref[...].astype(F32).astype(BF16)


def ordered_gate(mask, chip_class):
    tokens, latents = mask.shape
    rows = tokens // 16

    def source(r, l0, class_ref):
        return (4 * l0 + lax.rem(class_ref[0] + r + 2 * l0, 4), 0)

    return pl.pallas_call(
        gate_kernel,
        out_shape=jax.ShapeDtypeStruct((tokens, latents), BF16),
        grid_spec=pltpu.PrefetchScalarGridSpec(
            num_scalar_prefetch=1,
            grid=(4, 4),
            in_specs=[pl.BlockSpec((rows, latents), source)],
            out_specs=pl.BlockSpec((rows, latents), lambda r, l0, class_ref: (4 * r + l0, 0)),
        ),
        cost_estimate=cost(0, mask),
        compiler_params=params(),
    )(chip_class, mask)


def encode_kernel(count, *refs):
    tokens, weight_ref, out_ref, joined = refs[:count], *refs[count:]
    rows = tokens[0].shape[0]

    @pl.when(pl.program_id(0) == 0)
    def _():
        for i, ref in enumerate(tokens):
            joined[i * rows : (i + 1) * rows, :] = ref[...]

    out_ref[...] = jnp.dot(joined[...], weight_ref[...], preferred_element_type=F32)


def encode(tokens, weight, block=256):
    rows, features = tokens[0].shape
    latents = weight.shape[1]
    total = rows * len(tokens)
    return pl.pallas_call(
        functools.partial(encode_kernel, len(tokens)),
        out_shape=jax.ShapeDtypeStruct((total, latents), F32),
        grid=(latents // block,),
        in_specs=[whole((rows, features))] * len(tokens)
        + [pl.BlockSpec((features, block), lambda i: (0, i))],
        out_specs=pl.BlockSpec((total, block), lambda i: (0, i)),
        scratch_shapes=[pltpu.VMEM((total, features), BF16)],
        cost_estimate=cost(2 * total * features * latents, *tokens, weight),
        compiler_params=params(),
    )(*tokens, weight)


def decode_kernel(count, pre_ref, other_ref, bias_ref, gate_ref, weight_ref, *refs):
    parts, code_ref, total_ref = refs[:count], *refs[count:]
    rows = parts[0].shape[0]

    @pl.when(pl.program_id(0) == 0)
    def _():
        code = (pre_ref[...] + other_ref[...] + bias_ref[...]) * gate_ref[...].astype(F32)
        code_ref[...] = code.astype(BF16)
        total_ref[...] = jnp.sum(code, axis=0, keepdims=True)

    partial = jnp.dot(code_ref[...], weight_ref[...], preferred_element_type=F32)
    for i, ref in enumerate(parts):
        ref[...] = partial[i * rows : (i + 1) * rows, :].astype(ref.dtype)


def decode(pre, other, bias, gate, first, weight, dtype, block=512):
    total, latents = pre.shape
    features = weight.shape[1]
    rows = CHIPS * 8 // 4
    count = total // rows
    gates = pl.BlockSpec((pl.Element(total), pl.Element(latents)), lambda i: (first * rows, 0))
    *parts, code, code_total = pl.pallas_call(
        functools.partial(decode_kernel, count),
        out_shape=[jax.ShapeDtypeStruct((rows, features), dtype)] * count
        + [jax.ShapeDtypeStruct((total, latents), BF16), jax.ShapeDtypeStruct((1, latents), F32)],
        grid=(features // block,),
        in_specs=[
            whole((total, latents)),
            whole((total, latents)),
            whole((1, latents)),
            gates,
            pl.BlockSpec((latents, block), lambda i: (0, i)),
        ],
        out_specs=[pl.BlockSpec((rows, block), lambda i: (0, i))] * count
        + [whole((total, latents)), whole((1, latents))],
        cost_estimate=cost(2 * total * features * latents, pre, other, weight),
        compiler_params=params(),
    )(pre, other, bias, gate, weight)
    return parts, code, code_total


def add_kernel(own_ref, a_ref, b_ref, c_ref, out_ref):
    total = own_ref[...] + a_ref[...].astype(F32) + b_ref[...].astype(F32) + c_ref[...].astype(F32)
    out_ref[...] = total.astype(out_ref.dtype)


def add_quarters(own, others, block=64):
    rows, features = own.shape
    spec = pl.BlockSpec((block, features), lambda i: (i, 0))
    return pl.pallas_call(
        add_kernel,
        out_shape=jax.ShapeDtypeStruct((rows, features), BF16),
        grid=(rows // block,),
        in_specs=[spec] * 4,
        out_specs=spec,
        cost_estimate=cost(0, own, *others),
        compiler_params=params(),
    )(own, *others)


def error_kernel(parts_ref, rows_ref, bias_ref, code_a_ref, code_b_ref, norm_ref, out_ref):
    count, own, features = parts_ref.shape
    total = parts_ref[0].astype(F32)
    for i in range(1, count):
        total = total + parts_ref[i].astype(F32)
    error = total + bias_ref[...] - rows_ref[...].astype(F32)
    sparse = (code_a_ref[...] + code_b_ref[...]) * norm_ref[...]
    square = jnp.sum(jnp.sum(error * error, axis=0, keepdims=True), axis=1, keepdims=True)
    loss = 0.5 * square + SPARSITY * jnp.sum(sparse, axis=1, keepdims=True)
    loss = jnp.broadcast_to(loss, (own, EXTRA))
    high = loss.astype(BF16).astype(F32)
    middle = (loss - high).astype(BF16).astype(F32)
    low = loss - high - middle
    lane = lax.broadcasted_iota(jnp.int32, (own, EXTRA), 1)
    row = lax.broadcasted_iota(jnp.int32, (own, EXTRA), 0)
    terms = jnp.where(lane == 0, high, jnp.where(lane == 1, middle, jnp.where(lane == 2, low, 0.0)))
    terms = jnp.where(row == 0, terms, 0.0)
    sent = error.astype(BF16)
    terms = terms.astype(BF16)
    for i in range(count):
        out_ref[i, :, :features] = sent
        out_ref[i, :, features:] = terms


def error_blocks(parts, rows, bias, code_a, code_b, norm):
    count, own, features = parts.shape
    return pl.pallas_call(
        error_kernel,
        out_shape=jax.ShapeDtypeStruct((count, own, features + EXTRA), BF16),
        compiler_params=params(),
    )(parts, rows, bias, code_a, code_b, norm)


def code_grad_kernel(count, *refs):
    errors, norm_ref, weight_ref, out_ref, joined = refs[:count], *refs[count:]
    rows = errors[0].shape[0]
    features = weight_ref.shape[1]

    @pl.when(pl.program_id(0) == 0)
    def _():
        for i, ref in enumerate(errors):
            joined[i * rows : (i + 1) * rows, :] = ref[:, :features]

    out_ref[...] = (
        lax.dot_general(
            joined[...], weight_ref[...], (((1,), (1,)), ((), ())), preferred_element_type=F32
        )
        + SPARSITY * norm_ref[...]
    )


def code_gradient(errors, norm, weight, block=256):
    rows, width = errors[0].shape
    latents, features = weight.shape
    total = rows * len(errors)
    return pl.pallas_call(
        functools.partial(code_grad_kernel, len(errors)),
        out_shape=jax.ShapeDtypeStruct((total, latents), F32),
        grid=(latents // block,),
        in_specs=[whole((rows, width))] * len(errors)
        + [
            pl.BlockSpec((1, block), lambda i: (0, i)),
            pl.BlockSpec((block, features), lambda i: (i, 0)),
        ],
        out_specs=pl.BlockSpec((total, block), lambda i: (0, i)),
        scratch_shapes=[pltpu.VMEM((total, features), BF16)],
        cost_estimate=cost(2 * total * features * latents, *errors, weight),
        compiler_params=params(),
    )(*errors, norm, weight)


def loss_kernel(rows_per_chip, *refs):
    errors, out_ref = refs[:-1], refs[-1]
    total = jnp.zeros((1, EXTRA), F32)
    for ref in errors:
        total = total + jnp.sum(ref[...].astype(F32), axis=0, keepdims=True)
    out_ref[...] = jnp.broadcast_to(jnp.sum(total, axis=1, keepdims=True), out_ref.shape)


def layer_loss(errors, features):
    rows = errors[0].shape[0]
    spec = pl.BlockSpec((rows, EXTRA), lambda i: (0, features // EXTRA))
    return pl.pallas_call(
        functools.partial(loss_kernel, 8),
        out_shape=jax.ShapeDtypeStruct((8, EXTRA), F32),
        grid=(1,),
        in_specs=[spec] * len(errors),
        out_specs=whole((8, EXTRA)),
        compiler_params=params(),
    )(*errors)


def transpose_kernel(*refs):
    parts, out_ref = refs[:-1], refs[-1]
    start = 0
    for ref in parts:
        rows = ref.shape[0]
        out_ref[:, start : start + rows] = ref[...].T
        start += rows


def transposed(parts, block=512):
    width = parts[0].shape[1]
    total = sum(x.shape[0] for x in parts)
    return pl.pallas_call(
        transpose_kernel,
        out_shape=jax.ShapeDtypeStruct((width, total), BF16),
        grid=(width // block,),
        in_specs=[pl.BlockSpec((x.shape[0], block), lambda i: (0, i)) for x in parts],
        out_specs=pl.BlockSpec((block, total), lambda i: (i, 0)),
        cost_estimate=cost(0, *parts, *parts),
        compiler_params=params(),
    )(*parts)


def grad_dec_kernel(code_ref, e0, e1, e2, e3, scale_ref, weight_ref, out_ref, joined):
    rows = e0.shape[0]
    features = weight_ref.shape[1]

    @pl.when(pl.program_id(0) == 0)
    def _():
        for i, ref in enumerate((e0, e1, e2, e3)):
            joined[i * rows : (i + 1) * rows, :] = ref[:, :features]

    grad = jnp.dot(code_ref[...], joined[...], preferred_element_type=F32)
    shrink = scale_ref[:, :1] * weight_ref[...].astype(F32)
    out_ref[...] = (grad + shrink).astype(BF16)


def grad_decoder(code_t, errors, scale, weight, block=256):
    latents, features = weight.shape
    tokens = code_t.shape[1]
    rows, width = errors[0].shape
    return pl.pallas_call(
        grad_dec_kernel,
        out_shape=jax.ShapeDtypeStruct((latents, features), BF16),
        grid=(latents // block,),
        in_specs=[pl.BlockSpec((block, tokens), lambda i: (i, 0))]
        + [whole((rows, width))] * 4
        + [
            pl.BlockSpec((block, 128), lambda i: (i, 0)),
            pl.BlockSpec((block, features), lambda i: (i, 0)),
        ],
        out_specs=pl.BlockSpec((block, features), lambda i: (i, 0)),
        scratch_shapes=[pltpu.VMEM((tokens, features), BF16)],
        cost_estimate=cost(2 * tokens * features * latents, code_t, *errors, weight, weight),
        compiler_params=params(),
    )(code_t, *errors, scale, weight)


def grad_enc_kernel(token_ref, a_own, b_own, a_rest, b_rest, gate_ref, out_ref, pre_grad):
    rows = a_own.shape[0]

    @pl.when(pl.program_id(0) == 0)
    def _():
        own = (a_own[...] + b_own[...]) * gate_ref[:rows, :].astype(F32)
        pre_grad[:rows, :] = own.astype(BF16)
        rest = (a_rest[...] + b_rest[...]) * gate_ref[rows:, :].astype(F32)
        pre_grad[rows:, :] = rest.astype(BF16)

    out_ref[...] = jnp.dot(token_ref[...], pre_grad[...], preferred_element_type=F32).astype(BF16)


def grad_encoder(token_t, own, own_other, rest, rest_other, gate, block=256):
    features, tokens = token_t.shape
    latents = gate.shape[1]
    return pl.pallas_call(
        grad_enc_kernel,
        out_shape=jax.ShapeDtypeStruct((features, latents), BF16),
        grid=(features // block,),
        in_specs=[pl.BlockSpec((block, tokens), lambda i: (i, 0))]
        + [whole(own.shape)] * 2
        + [whole(rest.shape)] * 2
        + [whole(gate.shape)],
        out_specs=pl.BlockSpec((block, latents), lambda i: (i, 0)),
        scratch_shapes=[pltpu.VMEM((tokens, latents), BF16)],
        compiler_params=params(),
    )(token_t, own, own_other, rest, rest_other, gate)


def per_device(activations, enc_weight, enc_bias, dec_weight, dec_bias, active_mask):
    rows = activations[0]
    encoder = enc_weight[0]
    decoder = dec_weight[0]
    own, features = rows.shape
    tokens, latents = active_mask.shape
    members = CHIPS // 4
    quarter = members * own
    chip_class = lax.rem(lax.axis_index("latent_1") + 2 * lax.axis_index("latent_0"), 4)
    bias = enc_bias[None]

    q0 = class_exchange(jnp.broadcast_to(rows[None], (members, own, features)))
    q0 = q0.reshape(quarter, features)
    q123 = from_neighbours(q0)
    pre0 = encode([q0], encoder)
    other0 = swap_layers(pre0)
    gate = ordered_gate(active_mask, chip_class[None].astype(jnp.int32))
    dec_float = decoder.astype(F32)
    row_norm = jnp.sqrt(jnp.sum(dec_float * dec_float, axis=1) + 1e-06)
    q123, pre0, gate, row_norm = lax.optimization_barrier((q123, pre0, gate, row_norm))
    pre123 = encode(q123, encoder)
    other123 = swap_layers(pre123)

    parts, code123, total123 = decode(pre123, other123, bias, gate, 1, decoder, BF16)
    received = to_neighbours(parts)
    (part0,), code0, total0 = decode(pre0, other0, bias, gate, 0, decoder, F32)
    token_t = transposed([q0, *q123])
    received, part0, token_t = lax.optimization_barrier((received, part0, token_t))
    partial = add_quarters(part0, received)
    parts = class_exchange(partial.reshape(members, own, features))
    sent = error_blocks(parts, rows, dec_bias, total0, total123, row_norm[None])

    e0 = class_exchange(sent).reshape(quarter, features + EXTRA)
    e123 = from_neighbours(e0)
    norm = row_norm[None]
    grad0 = code_gradient([e0], norm, decoder)
    grad_other0 = swap_layers(grad0)
    code_t = transposed([code0, code123])
    scale = SPARSITY * (total0 + total123)[0] / row_norm
    scale = jnp.broadcast_to(scale[:, None], (latents, 128))
    e123, grad0, code_t, scale = lax.optimization_barrier((e123, grad0, code_t, scale))
    grad123 = code_gradient(e123, norm, decoder)
    grad_other123 = swap_layers(grad123)
    loss = layer_loss([e0, *e123], features)
    loss = (loss + swap_layers(loss))[0, 0]
    grad_dec = grad_decoder(code_t, [e0, *e123], scale, decoder)
    grad_enc = grad_encoder(token_t, grad0, grad_other0, grad123, grad_other123, gate)
    return (grad_enc[None], grad_dec[None], loss / (tokens * features))


def solution(mesh):
    torus = Mesh(
        mesh.devices.reshape(mesh.shape["layer"], SIDE, SIDE, SIDE),
        ("layer", *LATENT),
    )
    placed = (
        P("layer", LATENT, None),
        P("layer", None, LATENT),
        P(LATENT),
        P("layer", LATENT, None),
        P("layer", None),
        P(None, LATENT),
    )
    return jax.shard_map(
        per_device,
        mesh=torus,
        in_specs=placed,
        out_specs=(P("layer", None, LATENT), P("layer", LATENT, None), P()),
        check_vma=False,
    )
```

```python
import jax
import jax.numpy as jnp
from jax import lax
from jax.experimental import pallas as pl
from jax.experimental.pallas import tpu as pltpu
from jax.sharding import Mesh
from jax.sharding import PartitionSpec as P

LATENT = ("latent_0", "latent_1", "latent_2")
EVERY = ("layer", *LATENT)
SIDE = 4
CHIPS = SIDE**3
SPARSITY = 0.4
EXTRA = 128
MIB = 1 << 20
F32 = jnp.float32
BF16 = jnp.bfloat16

STEPS = (
    ((0, 0, 1), (-1, 0, 0), (0, 0, -1)),
    ((0, 1, 0), (1, 0, 0), (0, -1, 0)),
)


def class_groups():
    groups = [[] for _ in range(SIDE)]
    for chip in range(CHIPS):
        l0, l1, l2 = chip // 16, chip // 4 % 4, chip % 4
        groups[(l1 + 2 * l0 + l2) % SIDE].append(chip)
    return groups


def moved(quarter, sign):
    pairs = []
    for layer, steps in enumerate(STEPS):
        for chip in range(CHIPS):
            place = chip // 16, chip // 4 % 4, chip % 4
            target = [(p + sign * d) % SIDE for p, d in zip(place, steps[quarter - 1])]
            target = target[0] * 16 + target[1] * 4 + target[2]
            pairs.append((layer * CHIPS + chip, layer * CHIPS + target))
    return pairs


def class_exchange(x):
    return lax.all_to_all(x, LATENT, 0, 0, axis_index_groups=class_groups(), tiled=True)


def from_neighbours(x):
    return [lax.ppermute(x, EVERY, moved(r, -1)) for r in (1, 2, 3)]


def to_neighbours(parts):
    return [lax.ppermute(x, EVERY, moved(r, 1)) for r, x in zip((1, 2, 3), parts)]


def swap_layers(x):
    return lax.ppermute(x, "layer", [(0, 1), (1, 0)])


def params(mib=16):
    return pltpu.CompilerParams(vmem_limit_bytes=mib * MIB)


def cost(flops, *arrays):
    size = sum(a.size * a.dtype.itemsize for a in arrays)
    return pl.CostEstimate(flops=flops, bytes_accessed=size, transcendentals=0)


def whole(shape):
    return pl.BlockSpec(shape, lambda *_: (0,) * len(shape))


def gate_kernel(order_ref, mask_ref, gate_ref):
    own = 8
    blocks = gate_ref.shape[0] // own
    first = pl.program_id(0) * blocks
    for i in range(0, blocks, 2):
        pair = [
            mask_ref[pl.ds(pl.multiple_of(order_ref[first + j] * own, own), own), :]
            for j in (i, i + 1)
        ]
        gate_ref[i * own : (i + 2) * own, :] = jnp.concatenate(pair).astype(F32).astype(BF16)


def ordered_gate(mask, place):
    tokens, latents = mask.shape
    l0, l1, l2 = place
    index = jnp.arange(CHIPS, dtype=jnp.int32)
    column = index % 16
    row_class = l1 + 2 * l0 + l2 + index // 16
    order = 4 * column + (row_class - column % 4 - 2 * (column // 4) + 12) % 4
    return pl.pallas_call(
        gate_kernel,
        out_shape=jax.ShapeDtypeStruct((tokens, latents), BF16),
        grid_spec=pltpu.PrefetchScalarGridSpec(
            num_scalar_prefetch=1,
            grid=(4,),
            in_specs=[pl.BlockSpec((tokens, latents), lambda i, order_ref: (0, 0))],
            out_specs=pl.BlockSpec((tokens // 4, latents), lambda i, order_ref: (i, 0)),
        ),
        cost_estimate=cost(0, mask),
        compiler_params=params(),
    )(order.astype(jnp.int32), mask)


def add_kernel(own_ref, a_ref, b_ref, c_ref, out_ref):
    total = own_ref[...] + a_ref[...].astype(F32) + b_ref[...].astype(F32) + c_ref[...].astype(F32)
    out_ref[...] = total.astype(out_ref.dtype)


def add_quarters(own, others, block=64):
    rows, features = own.shape
    spec = pl.BlockSpec((block, features), lambda i: (i, 0))
    return pl.pallas_call(
        add_kernel,
        out_shape=jax.ShapeDtypeStruct((rows, features), BF16),
        grid=(rows // block,),
        in_specs=[spec] * 4,
        out_specs=spec,
        cost_estimate=cost(0, own, *others),
        compiler_params=params(),
    )(own, *others)


def error_kernel(parts_ref, rows_ref, bias_ref, code_a_ref, code_b_ref, norm_ref, out_ref):
    count, own, features = parts_ref.shape
    total = parts_ref[0].astype(F32)
    for i in range(1, count):
        total = total + parts_ref[i].astype(F32)
    error = total + bias_ref[...] - rows_ref[...].astype(F32)
    sparse = (code_a_ref[...] + code_b_ref[...]) * norm_ref[...]
    square = jnp.sum(jnp.sum(error * error, axis=0, keepdims=True), axis=1, keepdims=True)
    loss = 0.5 * square + SPARSITY * jnp.sum(sparse, axis=1, keepdims=True)
    loss = jnp.broadcast_to(loss, (own, EXTRA))
    high = loss.astype(BF16).astype(F32)
    middle = (loss - high).astype(BF16).astype(F32)
    low = loss - high - middle
    lane = lax.broadcasted_iota(jnp.int32, (own, EXTRA), 1)
    row = lax.broadcasted_iota(jnp.int32, (own, EXTRA), 0)
    terms = jnp.where(lane == 0, high, jnp.where(lane == 1, middle, jnp.where(lane == 2, low, 0.0)))
    terms = jnp.where(row == 0, terms, 0.0)
    sent = error.astype(BF16)
    terms = terms.astype(BF16)
    for i in range(count):
        out_ref[i, :, :features] = sent
        out_ref[i, :, features:] = terms


def error_blocks(parts, rows, bias, code_a, code_b, norm):
    count, own, features = parts.shape
    return pl.pallas_call(
        error_kernel,
        out_shape=jax.ShapeDtypeStruct((count, own, features + EXTRA), BF16),
        compiler_params=params(),
    )(parts, rows, bias, code_a, code_b, norm)


def code_gradient(error, norm, weight):
    grad = jnp.einsum("td,fd->tf", error, weight, preferred_element_type=F32)
    return grad + SPARSITY * norm


def loss_kernel(*refs):
    errors, out_ref = refs[:-1], refs[-1]
    total = jnp.zeros((1, EXTRA), F32)
    for ref in errors:
        total = total + jnp.sum(ref[...].astype(F32), axis=0, keepdims=True)
    out_ref[0, 0] = jnp.sum(total)


def layer_loss(errors, features):
    rows = errors[0].shape[0]
    spec = pl.BlockSpec((rows, EXTRA), lambda i: (0, features // EXTRA))
    loss = pl.pallas_call(
        loss_kernel,
        out_shape=jax.ShapeDtypeStruct((1, 1), F32),
        grid=(1,),
        in_specs=[spec] * len(errors),
        out_specs=pl.BlockSpec(memory_space=pltpu.SMEM),
        compiler_params=params(),
    )(*errors)
    return loss[0, 0]


def transpose_kernel(*refs):
    parts, out_ref = refs[:-1], refs[-1]
    start = 0
    for ref in parts:
        rows = ref.shape[0]
        out_ref[:, start : start + rows] = ref[...].T
        start += rows


def transposed(parts, block=512):
    width = parts[0].shape[1]
    total = sum(x.shape[0] for x in parts)
    return pl.pallas_call(
        transpose_kernel,
        out_shape=jax.ShapeDtypeStruct((width, total), BF16),
        grid=(width // block,),
        in_specs=[pl.BlockSpec((x.shape[0], block), lambda i: (0, i)) for x in parts],
        out_specs=pl.BlockSpec((block, total), lambda i: (i, 0)),
        cost_estimate=cost(0, *parts, *parts),
        compiler_params=params(),
    )(*parts)


def grad_dec_kernel(code_ref, e0, e1, e2, e3, scale_ref, weight_ref, out_ref, joined):
    rows = e0.shape[0]
    features = weight_ref.shape[1]

    @pl.when(pl.program_id(0) == 0)
    def _():
        for i, ref in enumerate((e0, e1, e2, e3)):
            joined[i * rows : (i + 1) * rows, :] = ref[:, :features]

    grad = jnp.dot(code_ref[...], joined[...], preferred_element_type=F32)
    shrink = scale_ref[:, :1] * weight_ref[...].astype(F32)
    out_ref[...] = (grad + shrink).astype(BF16)


def grad_decoder(code_t, errors, scale, weight, block=256):
    latents, features = weight.shape
    tokens = code_t.shape[1]
    rows, width = errors[0].shape
    return pl.pallas_call(
        grad_dec_kernel,
        out_shape=jax.ShapeDtypeStruct((latents, features), BF16),
        grid=(latents // block,),
        in_specs=[pl.BlockSpec((block, tokens), lambda i: (i, 0))]
        + [whole((rows, width))] * 4
        + [
            pl.BlockSpec((block, 128), lambda i: (i, 0)),
            pl.BlockSpec((block, features), lambda i: (i, 0)),
        ],
        out_specs=pl.BlockSpec((block, features), lambda i: (i, 0)),
        scratch_shapes=[pltpu.VMEM((tokens, features), BF16)],
        cost_estimate=cost(2 * tokens * features * latents, code_t, *errors, weight, weight),
        compiler_params=params(),
    )(code_t, *errors, scale, weight)


def grad_enc_kernel(token_ref, pre_grad_ref, out_ref):
    out_ref[...] = jnp.dot(
        token_ref[...], pre_grad_ref[...], preferred_element_type=F32
    ).astype(BF16)


def grad_encoder(token_t, pre_grad, block=512):
    features, tokens = token_t.shape
    latents = pre_grad.shape[1]
    return pl.pallas_call(
        grad_enc_kernel,
        out_shape=jax.ShapeDtypeStruct((features, latents), BF16),
        grid=(features // block,),
        in_specs=[pl.BlockSpec((block, tokens), lambda i: (i, 0)), whole(pre_grad.shape)],
        out_specs=pl.BlockSpec((block, latents), lambda i: (i, 0)),
        cost_estimate=cost(2 * tokens * features * latents, token_t, token_t, pre_grad),
        compiler_params=params(),
    )(token_t, pre_grad)


def per_device(activations, enc_weight, enc_bias, dec_weight, dec_bias, active_mask):
    rows = activations[0]
    encoder = enc_weight[0]
    decoder = dec_weight[0]
    own, features = rows.shape
    tokens, latents = active_mask.shape
    members = CHIPS // 4
    quarter = members * own
    bias = enc_bias[None]

    q0 = class_exchange(jnp.broadcast_to(rows[None], (members, own, features)))
    q0 = q0.reshape(quarter, features)
    place = [lax.axis_index(name) for name in LATENT]
    q0, active_mask, decoder, place = lax.optimization_barrier(
        (q0, active_mask, decoder, place)
    )
    q123 = from_neighbours(q0)
    pre0 = jnp.dot(q0, encoder, preferred_element_type=F32)
    other0 = swap_layers(pre0)
    gate = ordered_gate(active_mask, place)
    dec_float = decoder.astype(F32)
    row_norm = jnp.sqrt(jnp.sum(dec_float * dec_float, axis=1) + 1e-06)
    q123, pre0, gate, row_norm = lax.optimization_barrier((q123, pre0, gate, row_norm))
    pre123 = jnp.dot(jnp.concatenate(q123), encoder, preferred_element_type=F32)
    other123 = swap_layers(pre123)

    latent_code = (pre123 + other123 + bias) * gate[quarter:].astype(F32)
    total123 = jnp.sum(latent_code, axis=0, keepdims=True)
    code123 = latent_code.astype(BF16)
    parts = jnp.dot(code123, decoder, preferred_element_type=F32).astype(BF16)
    parts, all_tokens = lax.optimization_barrier((parts, [q0, *q123]))
    received = to_neighbours(parts.reshape(3, quarter, features))
    latent_code = (pre0 + other0 + bias) * gate[:quarter].astype(F32)
    total0 = jnp.sum(latent_code, axis=0, keepdims=True)
    code0 = latent_code.astype(BF16)
    part0 = jnp.dot(code0, decoder, preferred_element_type=F32)
    token_t = transposed(all_tokens)
    code_t = transposed([code0, code123])
    received, part0, token_t, code_t = lax.optimization_barrier((received, part0, token_t, code_t))
    partial = add_quarters(part0, received)
    parts = class_exchange(partial.reshape(members, own, features))
    sent = error_blocks(parts, rows, dec_bias, total0, total123, row_norm[None])

    e0 = class_exchange(sent).reshape(quarter, features + EXTRA)
    e123 = from_neighbours(e0)
    norm = row_norm[None]
    grad0 = code_gradient(e0[:, :features], norm, decoder)
    grad_other0 = swap_layers(grad0)
    scale = SPARSITY * (total0 + total123)[0] / row_norm
    scale = jnp.broadcast_to(scale[:, None], (latents, 128))
    e123, grad0, code_t, scale = lax.optimization_barrier((e123, grad0, code_t, scale))
    grad123 = code_gradient(jnp.concatenate([x[:, :features] for x in e123]), norm, decoder)
    grad_other123 = swap_layers(grad123)
    loss = layer_loss([e0, *e123], features)
    loss = loss + swap_layers(loss)
    grad_dec = grad_decoder(code_t, [e0, *e123], scale, decoder)
    pre_grad0 = ((grad0 + grad_other0) * gate[:quarter].astype(F32)).astype(BF16)
    pre_grad123 = ((grad123 + grad_other123) * gate[quarter:].astype(F32)).astype(BF16)
    grad_enc = grad_encoder(token_t, jnp.concatenate([pre_grad0, pre_grad123]))
    return (grad_enc[None], grad_dec[None], loss / (tokens * features))


def solution(mesh):
    torus = Mesh(
        mesh.devices.reshape(mesh.shape["layer"], SIDE, SIDE, SIDE),
        ("layer", *LATENT),
    )
    placed = (
        P("layer", LATENT, None),
        P("layer", None, LATENT),
        P(LATENT),
        P("layer", LATENT, None),
        P("layer", None),
        P(None, LATENT),
    )
    return jax.shard_map(
        per_device,
        mesh=torus,
        in_specs=placed,
        out_specs=(P("layer", None, LATENT), P("layer", LATENT, None), P()),
        check_vma=False,
    )
```

```python
import jax
import jax.numpy as jnp
from jax import lax
from jax.experimental import pallas as pl
from jax.experimental.pallas import tpu as pltpu
from jax.sharding import Mesh
from jax.sharding import PartitionSpec as P

LATENT = ("latent_0", "latent_1", "latent_2")
EVERY = ("layer", *LATENT)
SIDE = 4
CHIPS = SIDE**3
SPARSITY = 0.4
EXTRA = 128
MIB = 1 << 20
F32 = jnp.float32
BF16 = jnp.bfloat16

STEPS = (
    ((0, 0, 1), (-1, 0, 0), (0, 0, -1)),
    ((0, 1, 0), (1, 0, 0), (0, -1, 0)),
)


def class_groups():
    groups = [[] for _ in range(SIDE)]
    for chip in range(CHIPS):
        l0, l1, l2 = chip // 16, chip // 4 % 4, chip % 4
        groups[(l1 + 2 * l0 + l2) % SIDE].append(chip)
    return groups


def moved(quarter, sign):
    pairs = []
    for layer, steps in enumerate(STEPS):
        for chip in range(CHIPS):
            place = chip // 16, chip // 4 % 4, chip % 4
            target = [(p + sign * d) % SIDE for p, d in zip(place, steps[quarter - 1])]
            target = target[0] * 16 + target[1] * 4 + target[2]
            pairs.append((layer * CHIPS + chip, layer * CHIPS + target))
    return pairs


def class_exchange(x):
    return lax.all_to_all(x, LATENT, 0, 0, axis_index_groups=class_groups(), tiled=True)


def from_neighbours(x):
    return [lax.ppermute(x, EVERY, moved(r, -1)) for r in (1, 2, 3)]


def to_neighbours(parts):
    return [lax.ppermute(x, EVERY, moved(r, 1)) for r, x in zip((1, 2, 3), parts)]


def swap_layers(x):
    return lax.ppermute(x, "layer", [(0, 1), (1, 0)])


def params(mib=16):
    return pltpu.CompilerParams(vmem_limit_bytes=mib * MIB)


def cost(flops, *arrays):
    size = sum(a.size * a.dtype.itemsize for a in arrays)
    return pl.CostEstimate(flops=flops, bytes_accessed=size, transcendentals=0)


def whole(shape):
    return pl.BlockSpec(shape, lambda *_: (0,) * len(shape))


def gate_kernel(order_ref, mask_ref, gate_ref):
    own = 8
    blocks = gate_ref.shape[0] // own
    first = pl.program_id(0) * blocks
    for i in range(0, blocks, 2):
        pair = [
            mask_ref[pl.ds(pl.multiple_of(order_ref[first + j] * own, own), own), :]
            for j in (i, i + 1)
        ]
        gate_ref[i * own : (i + 2) * own, :] = jnp.concatenate(pair).astype(F32).astype(BF16)


def ordered_gate(mask, place):
    tokens, latents = mask.shape
    l0, l1, l2 = place
    index = jnp.arange(CHIPS, dtype=jnp.int32)
    column = index % 16
    row_class = l1 + 2 * l0 + l2 + index // 16
    order = 4 * column + (row_class - column % 4 - 2 * (column // 4) + 12) % 4
    return pl.pallas_call(
        gate_kernel,
        out_shape=jax.ShapeDtypeStruct((tokens, latents), BF16),
        grid_spec=pltpu.PrefetchScalarGridSpec(
            num_scalar_prefetch=1,
            grid=(4,),
            in_specs=[pl.BlockSpec((tokens, latents), lambda i, order_ref: (0, 0))],
            out_specs=pl.BlockSpec((tokens // 4, latents), lambda i, order_ref: (i, 0)),
        ),
        cost_estimate=cost(0, mask),
        compiler_params=params(),
    )(order.astype(jnp.int32), mask)


def add_kernel(own_ref, a_ref, b_ref, c_ref, out_ref):
    total = own_ref[...] + a_ref[...].astype(F32) + b_ref[...].astype(F32) + c_ref[...].astype(F32)
    out_ref[...] = total.astype(out_ref.dtype)


def add_quarters(own, others, block=64):
    rows, features = own.shape
    spec = pl.BlockSpec((block, features), lambda i: (i, 0))
    return pl.pallas_call(
        add_kernel,
        out_shape=jax.ShapeDtypeStruct((rows, features), BF16),
        grid=(rows // block,),
        in_specs=[spec] * 4,
        out_specs=spec,
        cost_estimate=cost(0, own, *others),
        compiler_params=params(),
    )(own, *others)


def error_kernel(parts_ref, rows_ref, bias_ref, code_a_ref, code_b_ref, norm_ref, out_ref):
    count, own, features = parts_ref.shape
    total = parts_ref[0].astype(F32)
    for i in range(1, count):
        total = total + parts_ref[i].astype(F32)
    error = total + bias_ref[...] - rows_ref[...].astype(F32)
    sparse = (code_a_ref[...] + code_b_ref[...]) * norm_ref[...]
    square = jnp.sum(jnp.sum(error * error, axis=0, keepdims=True), axis=1, keepdims=True)
    loss = 0.5 * square + SPARSITY * jnp.sum(sparse, axis=1, keepdims=True)
    loss = jnp.broadcast_to(loss, (own, EXTRA))
    high = loss.astype(BF16).astype(F32)
    middle = (loss - high).astype(BF16).astype(F32)
    low = loss - high - middle
    lane = lax.broadcasted_iota(jnp.int32, (own, EXTRA), 1)
    row = lax.broadcasted_iota(jnp.int32, (own, EXTRA), 0)
    terms = jnp.where(lane == 0, high, jnp.where(lane == 1, middle, jnp.where(lane == 2, low, 0.0)))
    terms = jnp.where(row == 0, terms, 0.0)
    sent = error.astype(BF16)
    terms = terms.astype(BF16)
    for i in range(count):
        out_ref[i, :, :features] = sent
        out_ref[i, :, features:] = terms


def error_blocks(parts, rows, bias, code_a, code_b, norm):
    count, own, features = parts.shape
    return pl.pallas_call(
        error_kernel,
        out_shape=jax.ShapeDtypeStruct((count, own, features + EXTRA), BF16),
        compiler_params=params(),
    )(parts, rows, bias, code_a, code_b, norm)


def code_gradient(error, norm, weight):
    grad = jnp.einsum("td,fd->tf", error, weight, preferred_element_type=F32)
    return grad + SPARSITY * norm


def transpose_kernel(*refs):
    parts, out_ref = refs[:-1], refs[-1]
    start = 0
    for ref in parts:
        rows = ref.shape[0]
        out_ref[:, start : start + rows] = ref[...].T
        start += rows


def transposed(parts, block=512):
    width = parts[0].shape[1]
    total = sum(x.shape[0] for x in parts)
    return pl.pallas_call(
        transpose_kernel,
        out_shape=jax.ShapeDtypeStruct((width, total), BF16),
        grid=(width // block,),
        in_specs=[pl.BlockSpec((x.shape[0], block), lambda i: (0, i)) for x in parts],
        out_specs=pl.BlockSpec((block, total), lambda i: (i, 0)),
        cost_estimate=cost(0, *parts, *parts),
        compiler_params=params(),
    )(*parts)


def grad_dec_kernel(code_ref, e0, e1, e2, e3, scale_ref, weight_ref, out_ref, loss_ref, joined):
    rows = e0.shape[0]
    features = weight_ref.shape[1]

    @pl.when(pl.program_id(0) == 0)
    def _():
        loss = jnp.zeros((rows, EXTRA), F32)
        for i, ref in enumerate((e0, e1, e2, e3)):
            joined[i * rows : (i + 1) * rows, :] = ref[:, :features]
            loss = loss + ref[:, features:].astype(F32)
        loss = jnp.sum(jnp.sum(loss, axis=0, keepdims=True), axis=1, keepdims=True)
        loss_ref[...] = jnp.broadcast_to(loss, loss_ref.shape)

    grad = jnp.dot(code_ref[...], joined[...], preferred_element_type=F32)
    shrink = scale_ref[:, :1] * weight_ref[...].astype(F32)
    out_ref[...] = (grad + shrink).astype(BF16)


def grad_decoder(code_t, errors, scale, weight, block=256):
    latents, features = weight.shape
    tokens = code_t.shape[1]
    rows, width = errors[0].shape
    return pl.pallas_call(
        grad_dec_kernel,
        out_shape=(
            jax.ShapeDtypeStruct((latents, features), BF16),
            jax.ShapeDtypeStruct((8, EXTRA), F32),
        ),
        grid=(latents // block,),
        in_specs=[pl.BlockSpec((block, tokens), lambda i: (i, 0))]
        + [whole((rows, width))] * 4
        + [
            pl.BlockSpec((block, 128), lambda i: (i, 0)),
            pl.BlockSpec((block, features), lambda i: (i, 0)),
        ],
        out_specs=(
            pl.BlockSpec((block, features), lambda i: (i, 0)),
            whole((8, EXTRA)),
        ),
        scratch_shapes=[pltpu.VMEM((tokens, features), BF16)],
        cost_estimate=cost(2 * tokens * features * latents, code_t, *errors, weight, weight),
        compiler_params=params(),
    )(code_t, *errors, scale, weight)


def per_device(activations, enc_weight, enc_bias, dec_weight, dec_bias, active_mask):
    rows = activations[0]
    encoder = enc_weight[0]
    decoder = dec_weight[0]
    own, features = rows.shape
    tokens, latents = active_mask.shape
    members = CHIPS // 4
    quarter = members * own
    bias = enc_bias[None]

    place = [lax.axis_index(name) for name in LATENT]
    rows, place = lax.optimization_barrier((rows, place))
    q0 = class_exchange(jnp.broadcast_to(rows[None], (members, own, features)))
    q0 = q0.reshape(quarter, features)
    q0, active_mask, decoder, place = lax.optimization_barrier(
        (q0, active_mask, decoder, place)
    )
    q123 = from_neighbours(q0)
    pre0 = jnp.dot(q0, encoder, preferred_element_type=F32)
    other0 = swap_layers(pre0)
    gate = ordered_gate(active_mask, place)
    dec_float = decoder.astype(F32)
    row_norm = jnp.sqrt(jnp.sum(dec_float * dec_float, axis=1) + 1e-06)
    q123, pre0, gate, row_norm = lax.optimization_barrier((q123, pre0, gate, row_norm))
    pre123 = jnp.dot(jnp.concatenate(q123), encoder, preferred_element_type=F32)
    other123 = swap_layers(pre123)

    latent_code = (pre123 + other123 + bias) * gate[quarter:].astype(F32)
    total123 = jnp.sum(latent_code, axis=0, keepdims=True)
    code123 = latent_code.astype(BF16)
    parts = jnp.dot(code123, decoder, preferred_element_type=F32).astype(BF16)
    received = to_neighbours(parts.reshape(3, quarter, features))
    latent_code = (pre0 + other0 + bias) * gate[:quarter].astype(F32)
    total0 = jnp.sum(latent_code, axis=0, keepdims=True)
    code0 = latent_code.astype(BF16)
    part0 = jnp.dot(code0, decoder, preferred_element_type=F32)
    code_t = transposed([code0, code123])
    received, part0, code_t = lax.optimization_barrier((received, part0, code_t))
    partial = add_quarters(part0, received)
    parts = class_exchange(partial.reshape(members, own, features))
    sent = error_blocks(parts, rows, dec_bias, total0, total123, row_norm[None])

    e0 = class_exchange(sent).reshape(quarter, features + EXTRA)
    e0, all_tokens = lax.optimization_barrier((e0, [q0, *q123]))
    e123 = from_neighbours(e0)
    token_t = transposed(all_tokens)
    norm = row_norm[None]
    grad0 = code_gradient(e0[:, :features], norm, decoder)
    grad_other0 = swap_layers(grad0)
    scale = SPARSITY * (total0 + total123)[0] / row_norm
    scale = jnp.broadcast_to(scale[:, None], (latents, 128))
    e123, grad0, grad_other0, token_t, scale = lax.optimization_barrier(
        (e123, grad0, grad_other0, token_t, scale)
    )
    grad123 = code_gradient(jnp.concatenate([x[:, :features] for x in e123]), norm, decoder)
    grad_other123 = swap_layers(grad123)
    grad_dec, loss = grad_decoder(code_t, [e0, *e123], scale, decoder)
    loss = (loss + swap_layers(loss))[0, 0]
    pre_grad0 = ((grad0 + grad_other0) * gate[:quarter].astype(F32)).astype(BF16)
    pre_grad123 = ((grad123 + grad_other123) * gate[quarter:].astype(F32)).astype(BF16)
    pre_grad = jnp.concatenate([pre_grad0, pre_grad123])
    grad_enc = jnp.dot(token_t, pre_grad, preferred_element_type=F32).astype(BF16)
    return (grad_enc[None], grad_dec[None], loss / (tokens * features))


def solution(mesh):
    torus = Mesh(
        mesh.devices.reshape(mesh.shape["layer"], SIDE, SIDE, SIDE),
        ("layer", *LATENT),
    )
    placed = (
        P("layer", LATENT, None),
        P("layer", None, LATENT),
        P(LATENT),
        P("layer", LATENT, None),
        P("layer", None),
        P(None, LATENT),
    )
    return jax.shard_map(
        per_device,
        mesh=torus,
        in_specs=placed,
        out_specs=(P("layer", None, LATENT), P("layer", LATENT, None), P()),
        check_vma=False,
    )
```

```python
import jax
import jax.numpy as jnp
from jax import lax
from jax.experimental import pallas as pl
from jax.experimental.pallas import tpu as pltpu
from jax.sharding import Mesh
from jax.sharding import PartitionSpec as P

LATENT = ("latent_0", "latent_1", "latent_2")
EVERY = ("layer", *LATENT)
SIDE = 4
CHIPS = SIDE**3
SPARSITY = 0.4
EXTRA = 128
MIB = 1 << 20
F32 = jnp.float32
BF16 = jnp.bfloat16

STEPS = (
    ((0, 0, 1), (-1, 0, 0), (0, 0, -1)),
    ((0, 1, 0), (1, 0, 0), (0, -1, 0)),
)


def class_groups():
    groups = [[] for _ in range(SIDE)]
    for chip in range(CHIPS):
        l0, l1, l2 = chip // 16, chip // 4 % 4, chip % 4
        groups[(l1 + 2 * l0 + l2) % SIDE].append(chip)
    return groups


def moved(quarter, sign):
    pairs = []
    for layer, steps in enumerate(STEPS):
        for chip in range(CHIPS):
            place = chip // 16, chip // 4 % 4, chip % 4
            target = [(p + sign * d) % SIDE for p, d in zip(place, steps[quarter - 1])]
            target = target[0] * 16 + target[1] * 4 + target[2]
            pairs.append((layer * CHIPS + chip, layer * CHIPS + target))
    return pairs


def class_exchange(x):
    return lax.all_to_all(x, LATENT, 0, 0, axis_index_groups=class_groups(), tiled=True)


def from_neighbours(x):
    return [lax.ppermute(x, EVERY, moved(r, -1)) for r in (1, 2, 3)]


def to_neighbours(parts):
    return [lax.ppermute(x, EVERY, moved(r, 1)) for r, x in zip((1, 2, 3), parts)]


def swap_layers(x):
    return lax.ppermute(x, "layer", [(0, 1), (1, 0)])


def params(mib=16):
    return pltpu.CompilerParams(vmem_limit_bytes=mib * MIB)


def cost(flops, *arrays):
    size = sum(a.size * a.dtype.itemsize for a in arrays)
    return pl.CostEstimate(flops=flops, bytes_accessed=size, transcendentals=0)


def whole(shape):
    return pl.BlockSpec(shape, lambda *_: (0,) * len(shape))


def gate_kernel(order_ref, mask_ref, gate_ref):
    own = 8
    blocks = gate_ref.shape[0] // own
    first = pl.program_id(0) * blocks
    for i in range(0, blocks, 2):
        pair = [
            mask_ref[pl.ds(pl.multiple_of(order_ref[first + j] * own, own), own), :]
            for j in (i, i + 1)
        ]
        gate_ref[i * own : (i + 2) * own, :] = jnp.concatenate(pair).astype(F32).astype(BF16)


def ordered_gate(mask, place):
    tokens, latents = mask.shape
    l0, l1, l2 = place
    index = jnp.arange(CHIPS, dtype=jnp.int32)
    column = index % 16
    row_class = l1 + 2 * l0 + l2 + index // 16
    order = 4 * column + (row_class - column % 4 - 2 * (column // 4) + 12) % 4
    return pl.pallas_call(
        gate_kernel,
        out_shape=jax.ShapeDtypeStruct((tokens, latents), BF16),
        grid_spec=pltpu.PrefetchScalarGridSpec(
            num_scalar_prefetch=1,
            grid=(4,),
            in_specs=[pl.BlockSpec((tokens, latents), lambda i, order_ref: (0, 0))],
            out_specs=pl.BlockSpec((tokens // 4, latents), lambda i, order_ref: (i, 0)),
        ),
        cost_estimate=cost(0, mask),
        compiler_params=params(),
    )(order.astype(jnp.int32), mask)


def add_kernel(own_ref, a_ref, b_ref, c_ref, out_ref):
    total = own_ref[...] + a_ref[...].astype(F32) + b_ref[...].astype(F32) + c_ref[...].astype(F32)
    out_ref[...] = total.astype(out_ref.dtype)


def add_quarters(own, others, block=64):
    rows, features = own.shape
    spec = pl.BlockSpec((block, features), lambda i: (i, 0))
    return pl.pallas_call(
        add_kernel,
        out_shape=jax.ShapeDtypeStruct((rows, features), BF16),
        grid=(rows // block,),
        in_specs=[spec] * 4,
        out_specs=spec,
        cost_estimate=cost(0, own, *others),
        compiler_params=params(),
    )(own, *others)


def error_kernel(parts_ref, rows_ref, bias_ref, code_a_ref, code_b_ref, norm_ref, out_ref):
    count, own, features = parts_ref.shape
    total = parts_ref[0].astype(F32)
    for i in range(1, count):
        total = total + parts_ref[i].astype(F32)
    error = total + bias_ref[...] - rows_ref[...].astype(F32)
    sparse = (code_a_ref[...] + code_b_ref[...]) * norm_ref[...]
    square = jnp.sum(jnp.sum(error * error, axis=0, keepdims=True), axis=1, keepdims=True)
    loss = 0.5 * square + SPARSITY * jnp.sum(sparse, axis=1, keepdims=True)
    loss = jnp.broadcast_to(loss, (own, EXTRA))
    high = loss.astype(BF16).astype(F32)
    middle = (loss - high).astype(BF16).astype(F32)
    low = loss - high - middle
    lane = lax.broadcasted_iota(jnp.int32, (own, EXTRA), 1)
    row = lax.broadcasted_iota(jnp.int32, (own, EXTRA), 0)
    terms = jnp.where(lane == 0, high, jnp.where(lane == 1, middle, jnp.where(lane == 2, low, 0.0)))
    terms = jnp.where(row == 0, terms, 0.0)
    sent = error.astype(BF16)
    terms = terms.astype(BF16)
    for i in range(count):
        out_ref[i, :, :features] = sent
        out_ref[i, :, features:] = terms


def error_blocks(parts, rows, bias, code_a, code_b, norm):
    count, own, features = parts.shape
    return pl.pallas_call(
        error_kernel,
        out_shape=jax.ShapeDtypeStruct((count, own, features + EXTRA), BF16),
        compiler_params=params(),
    )(parts, rows, bias, code_a, code_b, norm)


def code_gradient(error, norm, weight):
    grad = jnp.einsum("td,fd->tf", error, weight, preferred_element_type=F32)
    return grad + SPARSITY * norm


def transpose_kernel(*refs):
    parts, out_ref = refs[:-1], refs[-1]
    start = 0
    for ref in parts:
        rows = ref.shape[0]
        out_ref[:, start : start + rows] = ref[...].T
        start += rows


def transposed(parts, block=512):
    width = parts[0].shape[1]
    total = sum(x.shape[0] for x in parts)
    return pl.pallas_call(
        transpose_kernel,
        out_shape=jax.ShapeDtypeStruct((width, total), BF16),
        grid=(width // block,),
        in_specs=[pl.BlockSpec((x.shape[0], block), lambda i: (0, i)) for x in parts],
        out_specs=pl.BlockSpec((block, total), lambda i: (i, 0)),
        cost_estimate=cost(0, *parts, *parts),
        compiler_params=params(),
    )(*parts)


def grad_dec_kernel(
    code_ref, e0, e1, e2, e3, total_a, total_b, norm_ref, weight_ref, out_ref, loss_ref, joined
):
    rows = e0.shape[0]
    features = weight_ref.shape[1]

    @pl.when(pl.program_id(0) == 0)
    def _():
        loss = jnp.zeros((rows, EXTRA), F32)
        for i, ref in enumerate((e0, e1, e2, e3)):
            joined[i * rows : (i + 1) * rows, :] = ref[:, :features]
            loss = loss + ref[:, features:].astype(F32)
        loss = jnp.sum(jnp.sum(loss, axis=0, keepdims=True), axis=1, keepdims=True)
        loss_ref[...] = jnp.broadcast_to(loss, loss_ref.shape)

    grad = jnp.dot(code_ref[...], joined[...], preferred_element_type=F32)
    scale = SPARSITY * (total_a[...] + total_b[...]) / norm_ref[...]
    scale = jnp.broadcast_to(scale, (128, scale.shape[1])).T
    shrink = scale[:, :1] * weight_ref[...].astype(F32)
    out_ref[...] = (grad + shrink).astype(BF16)


def grad_decoder(code_t, errors, terms, weight, block=512):
    latents, features = weight.shape
    tokens = code_t.shape[1]
    rows, width = errors[0].shape
    return pl.pallas_call(
        grad_dec_kernel,
        out_shape=(
            jax.ShapeDtypeStruct((latents, features), BF16),
            jax.ShapeDtypeStruct((8, EXTRA), F32),
        ),
        grid=(latents // block,),
        in_specs=[pl.BlockSpec((block, tokens), lambda i: (i, 0))]
        + [whole((rows, width))] * 4
        + [pl.BlockSpec((1, block), lambda i: (0, i))] * 3
        + [pl.BlockSpec((block, features), lambda i: (i, 0))],
        out_specs=(
            pl.BlockSpec((block, features), lambda i: (i, 0)),
            whole((8, EXTRA)),
        ),
        scratch_shapes=[pltpu.VMEM((tokens, features), BF16)],
        cost_estimate=cost(2 * tokens * features * latents, code_t, *errors, weight, weight),
        compiler_params=params(),
    )(code_t, *errors, *terms, weight)


def grad_enc_kernel(token_ref, pre_grad_ref, out_ref):
    out_ref[...] = jnp.dot(
        token_ref[...], pre_grad_ref[...], preferred_element_type=F32
    ).astype(BF16)


def grad_encoder(token_t, pre_grad, block=1024):
    features, tokens = token_t.shape
    latents = pre_grad.shape[1]
    return pl.pallas_call(
        grad_enc_kernel,
        out_shape=jax.ShapeDtypeStruct((features, latents), BF16),
        grid=(features // block,),
        in_specs=[pl.BlockSpec((block, tokens), lambda i: (i, 0)), whole(pre_grad.shape)],
        out_specs=pl.BlockSpec((block, latents), lambda i: (i, 0)),
        cost_estimate=cost(2 * tokens * features * latents, token_t, token_t, pre_grad),
        compiler_params=params(),
    )(token_t, pre_grad)


def per_device(activations, enc_weight, enc_bias, dec_weight, dec_bias, active_mask):
    rows = activations[0]
    encoder = enc_weight[0]
    decoder = dec_weight[0]
    own, features = rows.shape
    tokens, latents = active_mask.shape
    members = CHIPS // 4
    quarter = members * own
    bias = enc_bias[None]

    place = [lax.axis_index(name) for name in LATENT]
    rows, place = lax.optimization_barrier((rows, place))
    q0 = class_exchange(jnp.broadcast_to(rows[None], (members, own, features)))
    q0 = q0.reshape(quarter, features)
    q0, active_mask, decoder, place = lax.optimization_barrier(
        (q0, active_mask, decoder, place)
    )
    q123 = from_neighbours(q0)
    pre0 = jnp.dot(q0, encoder, preferred_element_type=F32)
    other0 = swap_layers(pre0)
    gate = ordered_gate(active_mask, place)
    dec_float = decoder.astype(F32)
    row_norm = jnp.sqrt(jnp.sum(dec_float * dec_float, axis=1) + 1e-06)
    q123, pre0, gate, row_norm = lax.optimization_barrier((q123, pre0, gate, row_norm))
    pre123 = jnp.dot(jnp.concatenate(q123), encoder, preferred_element_type=F32)
    other123 = swap_layers(pre123.astype(BF16)).astype(F32)

    latent_code = (pre123 + other123 + bias) * gate[quarter:].astype(F32)
    total123 = jnp.sum(latent_code, axis=0, keepdims=True)
    code123 = latent_code.astype(BF16)
    parts = jnp.dot(code123, decoder, preferred_element_type=F32).astype(BF16)
    received = to_neighbours(parts.reshape(3, quarter, features))
    latent_code = (pre0 + other0 + bias) * gate[:quarter].astype(F32)
    total0 = jnp.sum(latent_code, axis=0, keepdims=True)
    code0 = latent_code.astype(BF16)
    part0 = jnp.dot(code0, decoder, preferred_element_type=F32)
    code_t = transposed([code0, code123])
    received, part0, code_t = lax.optimization_barrier((received, part0, code_t))
    partial = add_quarters(part0, received)
    parts = class_exchange(partial.reshape(members, own, features))
    sent = error_blocks(parts, rows, dec_bias, total0, total123, row_norm[None])

    e0 = class_exchange(sent).reshape(quarter, features + EXTRA)
    e0, all_tokens = lax.optimization_barrier((e0, [q0, *q123]))
    e123 = from_neighbours(e0)
    token_t = transposed(all_tokens)
    norm = row_norm[None]
    grad0 = code_gradient(e0[:, :features], norm, decoder)
    grad_other0 = swap_layers(grad0)
    e123, grad0, grad_other0, token_t = lax.optimization_barrier(
        (e123, grad0, grad_other0, token_t)
    )
    grad123 = code_gradient(jnp.concatenate([x[:, :features] for x in e123]), norm, decoder)
    grad_other123 = swap_layers(grad123)
    grad_dec, loss = grad_decoder(code_t, [e0, *e123], (total0, total123, norm), decoder)
    other_loss = swap_layers(loss)
    pre_grad0 = ((grad0 + grad_other0) * gate[:quarter].astype(F32)).astype(BF16)
    pre_grad123 = ((grad123 + grad_other123) * gate[quarter:].astype(F32)).astype(BF16)
    pre_grad = jnp.concatenate([pre_grad0, pre_grad123])
    grad_enc = grad_encoder(token_t, pre_grad)
    grad_enc, loss, other_loss = lax.optimization_barrier((grad_enc, loss, other_loss))
    loss = (loss + other_loss)[0, 0]
    return (grad_enc[None], grad_dec[None], loss / (tokens * features))


def solution(mesh):
    torus = Mesh(
        mesh.devices.reshape(mesh.shape["layer"], SIDE, SIDE, SIDE),
        ("layer", *LATENT),
    )
    placed = (
        P("layer", LATENT, None),
        P("layer", None, LATENT),
        P(LATENT),
        P("layer", LATENT, None),
        P("layer", None),
        P(None, LATENT),
    )
    return jax.shard_map(
        per_device,
        mesh=torus,
        in_specs=placed,
        out_specs=(P("layer", None, LATENT), P("layer", LATENT, None), P()),
        check_vma=False,
    )
```

```python
import jax
import jax.numpy as jnp
from jax import lax
from jax.experimental import pallas as pl
from jax.experimental.pallas import tpu as pltpu
from jax.sharding import Mesh
from jax.sharding import PartitionSpec as P

LATENT = ("latent_0", "latent_1", "latent_2")
EVERY = ("layer", *LATENT)
SIDE = 4
CHIPS = SIDE**3
SPARSITY = 0.4
EXTRA = 128
MIB = 1 << 20
F32 = jnp.float32
BF16 = jnp.bfloat16

STEPS = (
    ((0, 0, 1), (-1, 0, 0), (0, 0, -1)),
    ((0, 1, 0), (1, 0, 0), (0, -1, 0)),
)


def class_groups():
    groups = [[] for _ in range(SIDE)]
    for chip in range(CHIPS):
        l0, l1, l2 = chip // 16, chip // 4 % 4, chip % 4
        groups[(l1 + 2 * l0 + l2) % SIDE].append(chip)
    return groups


def moved(quarter, sign):
    pairs = []
    for layer, steps in enumerate(STEPS):
        for chip in range(CHIPS):
            place = chip // 16, chip // 4 % 4, chip % 4
            target = [(p + sign * d) % SIDE for p, d in zip(place, steps[quarter - 1])]
            target = target[0] * 16 + target[1] * 4 + target[2]
            pairs.append((layer * CHIPS + chip, layer * CHIPS + target))
    return pairs


def class_exchange(x):
    return lax.all_to_all(x, LATENT, 0, 0, axis_index_groups=class_groups(), tiled=True)


def from_neighbours(x):
    return [lax.ppermute(x, EVERY, moved(r, -1)) for r in (1, 2, 3)]


def to_neighbours(parts):
    return [lax.ppermute(x, EVERY, moved(r, 1)) for r, x in zip((1, 2, 3), parts)]


def swap_layers(x):
    return lax.ppermute(x, "layer", [(0, 1), (1, 0)])


def params(mib=16):
    return pltpu.CompilerParams(vmem_limit_bytes=mib * MIB)


def cost(flops, *arrays):
    size = sum(a.size * a.dtype.itemsize for a in arrays)
    return pl.CostEstimate(flops=flops, bytes_accessed=size, transcendentals=0)


def whole(shape):
    return pl.BlockSpec(shape, lambda *_: (0,) * len(shape))


def gate_kernel(order_ref, mask_ref, gate_ref):
    own = 8
    blocks = gate_ref.shape[0] // own
    first = pl.program_id(0) * blocks
    for i in range(0, blocks, 2):
        pair = [
            mask_ref[pl.ds(pl.multiple_of(order_ref[first + j] * own, own), own), :]
            for j in (i, i + 1)
        ]
        gate_ref[i * own : (i + 2) * own, :] = jnp.concatenate(pair).astype(F32).astype(BF16)


def ordered_gate(mask, place):
    tokens, latents = mask.shape
    l0, l1, l2 = place
    index = jnp.arange(CHIPS, dtype=jnp.int32)
    column = index % 16
    row_class = l1 + 2 * l0 + l2 + index // 16
    order = 4 * column + (row_class - column % 4 - 2 * (column // 4) + 12) % 4
    return pl.pallas_call(
        gate_kernel,
        out_shape=jax.ShapeDtypeStruct((tokens, latents), BF16),
        grid_spec=pltpu.PrefetchScalarGridSpec(
            num_scalar_prefetch=1,
            grid=(4,),
            in_specs=[pl.BlockSpec((tokens, latents), lambda i, order_ref: (0, 0))],
            out_specs=pl.BlockSpec((tokens // 4, latents), lambda i, order_ref: (i, 0)),
        ),
        cost_estimate=cost(0, mask),
        compiler_params=params(),
    )(order.astype(jnp.int32), mask)


def add_kernel(own_ref, a_ref, b_ref, c_ref, out_ref):
    total = own_ref[...] + a_ref[...].astype(F32) + b_ref[...].astype(F32) + c_ref[...].astype(F32)
    out_ref[...] = total.astype(out_ref.dtype)


def add_quarters(own, others, block=64):
    rows, features = own.shape
    spec = pl.BlockSpec((block, features), lambda i: (i, 0))
    return pl.pallas_call(
        add_kernel,
        out_shape=jax.ShapeDtypeStruct((rows, features), BF16),
        grid=(rows // block,),
        in_specs=[spec] * 4,
        out_specs=spec,
        cost_estimate=cost(0, own, *others),
        compiler_params=params(),
    )(own, *others)


def error_kernel(parts_ref, rows_ref, bias_ref, code_a_ref, code_b_ref, norm_ref, out_ref):
    count, own, features = parts_ref.shape
    total = parts_ref[0].astype(F32)
    for i in range(1, count):
        total = total + parts_ref[i].astype(F32)
    error = total + bias_ref[...] - rows_ref[...].astype(F32)
    sparse = (code_a_ref[...] + code_b_ref[...]) * norm_ref[...]
    square = jnp.sum(jnp.sum(error * error, axis=0, keepdims=True), axis=1, keepdims=True)
    loss = 0.5 * square + SPARSITY * jnp.sum(sparse, axis=1, keepdims=True)
    loss = jnp.broadcast_to(loss, (own, EXTRA))
    high = loss.astype(BF16).astype(F32)
    middle = (loss - high).astype(BF16).astype(F32)
    low = loss - high - middle
    lane = lax.broadcasted_iota(jnp.int32, (own, EXTRA), 1)
    row = lax.broadcasted_iota(jnp.int32, (own, EXTRA), 0)
    terms = jnp.where(lane == 0, high, jnp.where(lane == 1, middle, jnp.where(lane == 2, low, 0.0)))
    terms = jnp.where(row == 0, terms, 0.0)
    sent = error.astype(BF16)
    terms = terms.astype(BF16)
    for i in range(count):
        out_ref[i, :, :features] = sent
        out_ref[i, :, features:] = terms


def error_blocks(parts, rows, bias, code_a, code_b, norm):
    count, own, features = parts.shape
    return pl.pallas_call(
        error_kernel,
        out_shape=jax.ShapeDtypeStruct((count, own, features + EXTRA), BF16),
        compiler_params=params(),
    )(parts, rows, bias, code_a, code_b, norm)


def code_gradient(error, norm, weight):
    grad = jnp.einsum("td,fd->tf", error, weight, preferred_element_type=F32)
    return grad + SPARSITY * norm


def transpose_kernel(*refs):
    parts, out_ref = refs[:-1], refs[-1]
    start = 0
    for ref in parts:
        rows = ref.shape[0]
        out_ref[:, start : start + rows] = ref[...].T
        start += rows


def transposed(parts, block=512):
    width = parts[0].shape[1]
    total = sum(x.shape[0] for x in parts)
    return pl.pallas_call(
        transpose_kernel,
        out_shape=jax.ShapeDtypeStruct((width, total), BF16),
        grid=(width // block,),
        in_specs=[pl.BlockSpec((x.shape[0], block), lambda i: (0, i)) for x in parts],
        out_specs=pl.BlockSpec((block, total), lambda i: (i, 0)),
        cost_estimate=cost(0, *parts, *parts),
        compiler_params=params(),
    )(*parts)


def grad_dec_kernel(
    code_ref, e0, e1, e2, e3, total_a, total_b, norm_ref, weight_ref, out_ref, loss_ref, joined
):
    rows = e0.shape[0]
    features = weight_ref.shape[1]

    @pl.when(pl.program_id(0) == 0)
    def _():
        loss = jnp.zeros((rows, EXTRA), F32)
        for i, ref in enumerate((e0, e1, e2, e3)):
            joined[i * rows : (i + 1) * rows, :] = ref[:, :features]
            loss = loss + ref[:, features:].astype(F32)
        loss = jnp.sum(jnp.sum(loss, axis=0, keepdims=True), axis=1, keepdims=True)
        loss_ref[...] = jnp.broadcast_to(loss, loss_ref.shape)

    grad = jnp.dot(code_ref[...], joined[...], preferred_element_type=F32)
    scale = SPARSITY * (total_a[...] + total_b[...]) / norm_ref[...]
    scale = jnp.broadcast_to(scale, (128, scale.shape[1])).T
    shrink = scale[:, :1] * weight_ref[...].astype(F32)
    out_ref[...] = (grad + shrink).astype(BF16)


def grad_decoder(code_t, errors, terms, weight, block=512):
    latents, features = weight.shape
    tokens = code_t.shape[1]
    rows, width = errors[0].shape
    return pl.pallas_call(
        grad_dec_kernel,
        out_shape=(
            jax.ShapeDtypeStruct((latents, features), BF16),
            jax.ShapeDtypeStruct((8, EXTRA), F32),
        ),
        grid=(latents // block,),
        in_specs=[pl.BlockSpec((block, tokens), lambda i: (i, 0))]
        + [whole((rows, width))] * 4
        + [pl.BlockSpec((1, block), lambda i: (0, i))] * 3
        + [pl.BlockSpec((block, features), lambda i: (i, 0))],
        out_specs=(
            pl.BlockSpec((block, features), lambda i: (i, 0)),
            whole((8, EXTRA)),
        ),
        scratch_shapes=[pltpu.VMEM((tokens, features), BF16)],
        cost_estimate=cost(2 * tokens * features * latents, code_t, *errors, weight, weight),
        compiler_params=params(),
    )(code_t, *errors, *terms, weight)


def grad_enc_kernel(token_ref, pre_grad_ref, out_ref):
    out_ref[...] = jnp.dot(
        token_ref[...], pre_grad_ref[...], preferred_element_type=F32
    ).astype(BF16)


def grad_encoder(token_t, pre_grad, block=1024):
    features, tokens = token_t.shape
    latents = pre_grad.shape[1]
    return pl.pallas_call(
        grad_enc_kernel,
        out_shape=jax.ShapeDtypeStruct((features, latents), BF16),
        grid=(features // block,),
        in_specs=[pl.BlockSpec((block, tokens), lambda i: (i, 0)), whole(pre_grad.shape)],
        out_specs=pl.BlockSpec((block, latents), lambda i: (i, 0)),
        cost_estimate=cost(2 * tokens * features * latents, token_t, token_t, pre_grad),
        compiler_params=params(),
    )(token_t, pre_grad)


def per_device(activations, enc_weight, enc_bias, dec_weight, dec_bias, active_mask):
    rows = activations[0]
    encoder = enc_weight[0]
    decoder = dec_weight[0]
    own, features = rows.shape
    tokens, latents = active_mask.shape
    members = CHIPS // 4
    quarter = members * own
    bias = enc_bias[None]

    place = [lax.axis_index(name) for name in LATENT]
    rows, place = lax.optimization_barrier((rows, place))
    q0 = class_exchange(jnp.broadcast_to(rows[None], (members, own, features)))
    q0 = q0.reshape(quarter, features)
    q0, active_mask, decoder, place = lax.optimization_barrier(
        (q0, active_mask, decoder, place)
    )
    q123 = from_neighbours(q0)
    pre0 = jnp.dot(q0, encoder, preferred_element_type=F32)
    other0 = swap_layers(pre0)
    gate = ordered_gate(active_mask, place)
    dec_float = decoder.astype(F32)
    row_norm = jnp.sqrt(jnp.sum(dec_float * dec_float, axis=1) + 1e-06)
    q123, pre0, gate, row_norm = lax.optimization_barrier((q123, pre0, gate, row_norm))
    pre123 = jnp.dot(jnp.concatenate(q123), encoder, preferred_element_type=F32)
    other123 = swap_layers(pre123.astype(BF16)).astype(F32)

    latent_code = (pre123 + other123 + bias) * gate[quarter:].astype(F32)
    total123 = jnp.sum(latent_code, axis=0, keepdims=True)
    code123 = latent_code.astype(BF16)
    parts = jnp.dot(code123, decoder, preferred_element_type=F32).astype(BF16)
    received = to_neighbours(parts.reshape(3, quarter, features))
    latent_code = (pre0 + other0 + bias) * gate[:quarter].astype(F32)
    total0 = jnp.sum(latent_code, axis=0, keepdims=True)
    code0 = latent_code.astype(BF16)
    part0 = jnp.dot(code0, decoder, preferred_element_type=F32)
    code_t = transposed([code0, code123])
    received, part0, code_t = lax.optimization_barrier((received, part0, code_t))
    partial = add_quarters(part0, received)
    parts = class_exchange(partial.reshape(members, own, features))
    sent = error_blocks(parts, rows, dec_bias, total0, total123, row_norm[None])

    e0 = class_exchange(sent).reshape(quarter, features + EXTRA)
    e0, all_tokens = lax.optimization_barrier((e0, [q0, *q123]))
    e123 = from_neighbours(e0)
    token_t = transposed(all_tokens)
    norm = row_norm[None]
    grad0 = code_gradient(e0[:, :features], norm, decoder)
    grad_other0 = swap_layers(grad0)
    e123, grad0, grad_other0, token_t = lax.optimization_barrier(
        (e123, grad0, grad_other0, token_t)
    )
    grad123 = code_gradient(jnp.concatenate([x[:, :features] for x in e123]), norm, decoder)
    grad_other123 = swap_layers(grad123.astype(BF16)).astype(F32)
    grad_dec, loss = grad_decoder(code_t, [e0, *e123], (total0, total123, norm), decoder)
    other_loss = swap_layers(loss)
    pre_grad0 = ((grad0 + grad_other0) * gate[:quarter].astype(F32)).astype(BF16)
    pre_grad123 = ((grad123 + grad_other123) * gate[quarter:].astype(F32)).astype(BF16)
    pre_grad = jnp.concatenate([pre_grad0, pre_grad123])
    grad_enc = grad_encoder(token_t, pre_grad)
    grad_enc, loss, other_loss = lax.optimization_barrier((grad_enc, loss, other_loss))
    loss = (loss + other_loss)[0, 0]
    return (grad_enc[None], grad_dec[None], loss / (tokens * features))


def solution(mesh):
    torus = Mesh(
        mesh.devices.reshape(mesh.shape["layer"], SIDE, SIDE, SIDE),
        ("layer", *LATENT),
    )
    placed = (
        P("layer", LATENT, None),
        P("layer", None, LATENT),
        P(LATENT),
        P("layer", LATENT, None),
        P("layer", None),
        P(None, LATENT),
    )
    return jax.shard_map(
        per_device,
        mesh=torus,
        in_specs=placed,
        out_specs=(P("layer", None, LATENT), P("layer", LATENT, None), P()),
        check_vma=False,
    )
```

```python
import jax
import jax.numpy as jnp
from jax import lax
from jax.experimental import pallas as pl
from jax.experimental.pallas import tpu as pltpu
from jax.sharding import Mesh
from jax.sharding import PartitionSpec as P

LATENT = ("latent_0", "latent_1", "latent_2")
EVERY = ("layer", *LATENT)
SIDE = 4
CHIPS = SIDE**3
SPARSITY = 0.4
EXTRA = 128
MIB = 1 << 20
F32 = jnp.float32
BF16 = jnp.bfloat16

STEPS = (
    ((0, 0, 1), (-1, 0, 0), (0, 0, -1)),
    ((0, 1, 0), (1, 0, 0), (0, -1, 0)),
)


def class_groups():
    groups = [[] for _ in range(SIDE)]
    for chip in range(CHIPS):
        l0, l1, l2 = chip // 16, chip // 4 % 4, chip % 4
        groups[(l1 + 2 * l0 + l2) % SIDE].append(chip)
    return groups


def moved(quarter, sign):
    pairs = []
    for layer, steps in enumerate(STEPS):
        for chip in range(CHIPS):
            place = chip // 16, chip // 4 % 4, chip % 4
            target = [(p + sign * d) % SIDE for p, d in zip(place, steps[quarter - 1])]
            target = target[0] * 16 + target[1] * 4 + target[2]
            pairs.append((layer * CHIPS + chip, layer * CHIPS + target))
    return pairs


def class_exchange(x):
    return lax.all_to_all(x, LATENT, 0, 0, axis_index_groups=class_groups(), tiled=True)


def from_neighbours(x):
    return [lax.ppermute(x, EVERY, moved(r, -1)) for r in (1, 2, 3)]


def to_neighbours(parts):
    return [lax.ppermute(x, EVERY, moved(r, 1)) for r, x in zip((1, 2, 3), parts)]


def swap_layers(x):
    return lax.ppermute(x, "layer", [(0, 1), (1, 0)])


def params(mib=16):
    return pltpu.CompilerParams(vmem_limit_bytes=mib * MIB)


def cost(flops, *arrays):
    size = sum(a.size * a.dtype.itemsize for a in arrays)
    return pl.CostEstimate(flops=flops, bytes_accessed=size, transcendentals=0)


def whole(shape):
    return pl.BlockSpec(shape, lambda *_: (0,) * len(shape))


def gate_kernel(order_ref, mask_ref, gate_ref):
    own = 8
    blocks = gate_ref.shape[0] // own
    first = pl.program_id(0) * blocks
    for i in range(0, blocks, 2):
        pair = [
            mask_ref[pl.ds(pl.multiple_of(order_ref[first + j] * own, own), own), :]
            for j in (i, i + 1)
        ]
        gate_ref[i * own : (i + 2) * own, :] = jnp.concatenate(pair).astype(F32).astype(BF16)


def ordered_gate(mask, place):
    tokens, latents = mask.shape
    l0, l1, l2 = place
    index = jnp.arange(CHIPS, dtype=jnp.int32)
    column = index % 16
    row_class = l1 + 2 * l0 + l2 + index // 16
    order = 4 * column + (row_class - column % 4 - 2 * (column // 4) + 12) % 4
    return pl.pallas_call(
        gate_kernel,
        out_shape=jax.ShapeDtypeStruct((tokens, latents), BF16),
        grid_spec=pltpu.PrefetchScalarGridSpec(
            num_scalar_prefetch=1,
            grid=(4,),
            in_specs=[pl.BlockSpec((tokens, latents), lambda i, order_ref: (0, 0))],
            out_specs=pl.BlockSpec((tokens // 4, latents), lambda i, order_ref: (i, 0)),
        ),
        cost_estimate=cost(0, mask),
        compiler_params=params(),
    )(order.astype(jnp.int32), mask)


def add_kernel(own_ref, a_ref, b_ref, c_ref, out_ref):
    total = own_ref[...] + a_ref[...].astype(F32) + b_ref[...].astype(F32) + c_ref[...].astype(F32)
    out_ref[...] = total.astype(out_ref.dtype)


def add_quarters(own, others, block=64):
    rows, features = own.shape
    spec = pl.BlockSpec((block, features), lambda i: (i, 0))
    return pl.pallas_call(
        add_kernel,
        out_shape=jax.ShapeDtypeStruct((rows, features), BF16),
        grid=(rows // block,),
        in_specs=[spec] * 4,
        out_specs=spec,
        cost_estimate=cost(0, own, *others),
        compiler_params=params(),
    )(own, *others)


def error_kernel(parts_ref, rows_ref, bias_ref, code_a_ref, code_b_ref, norm_ref, out_ref):
    count, own, features = parts_ref.shape
    total = parts_ref[0].astype(F32)
    for i in range(1, count):
        total = total + parts_ref[i].astype(F32)
    error = total + bias_ref[...] - rows_ref[...].astype(F32)
    sparse = (code_a_ref[...] + code_b_ref[...]) * norm_ref[...]
    square = jnp.sum(jnp.sum(error * error, axis=0, keepdims=True), axis=1, keepdims=True)
    loss = 0.5 * square + SPARSITY * jnp.sum(sparse, axis=1, keepdims=True)
    loss = jnp.broadcast_to(loss, (own, EXTRA))
    high = loss.astype(BF16).astype(F32)
    middle = (loss - high).astype(BF16).astype(F32)
    low = loss - high - middle
    lane = lax.broadcasted_iota(jnp.int32, (own, EXTRA), 1)
    row = lax.broadcasted_iota(jnp.int32, (own, EXTRA), 0)
    terms = jnp.where(lane == 0, high, jnp.where(lane == 1, middle, jnp.where(lane == 2, low, 0.0)))
    terms = jnp.where(row == 0, terms, 0.0)
    sent = error.astype(BF16)
    terms = terms.astype(BF16)
    for i in range(count):
        out_ref[i, :, :features] = sent
        out_ref[i, :, features:] = terms


def error_blocks(parts, rows, bias, code_a, code_b, norm):
    count, own, features = parts.shape
    return pl.pallas_call(
        error_kernel,
        out_shape=jax.ShapeDtypeStruct((count, own, features + EXTRA), BF16),
        compiler_params=params(),
    )(parts, rows, bias, code_a, code_b, norm)


def code_gradient(error, norm, weight):
    grad = jnp.einsum("td,fd->tf", error, weight, preferred_element_type=F32)
    return grad + SPARSITY * norm


def transpose_kernel(*refs):
    parts, out_ref = refs[:-1], refs[-1]
    start = 0
    for ref in parts:
        rows = ref.shape[0]
        out_ref[:, start : start + rows] = ref[...].T
        start += rows


def transposed(parts, block=512):
    width = parts[0].shape[1]
    total = sum(x.shape[0] for x in parts)
    return pl.pallas_call(
        transpose_kernel,
        out_shape=jax.ShapeDtypeStruct((width, total), BF16),
        grid=(width // block,),
        in_specs=[pl.BlockSpec((x.shape[0], block), lambda i: (0, i)) for x in parts],
        out_specs=pl.BlockSpec((block, total), lambda i: (i, 0)),
        cost_estimate=cost(0, *parts, *parts),
        compiler_params=params(),
    )(*parts)


def grad_dec_kernel(
    code_ref, e0, e1, e2, e3, total_a, total_b, norm_ref, weight_ref, out_ref, loss_ref, joined
):
    rows = e0.shape[0]
    features = weight_ref.shape[1]

    @pl.when(pl.program_id(0) == 0)
    def _():
        loss = jnp.zeros((rows, EXTRA), F32)
        for i, ref in enumerate((e0, e1, e2, e3)):
            joined[i * rows : (i + 1) * rows, :] = ref[:, :features]
            loss = loss + ref[:, features:].astype(F32)
        loss = jnp.sum(jnp.sum(loss, axis=0, keepdims=True), axis=1, keepdims=True)
        loss_ref[...] = jnp.broadcast_to(loss, loss_ref.shape)

    grad = jnp.dot(code_ref[...], joined[...], preferred_element_type=F32)
    scale = SPARSITY * (total_a[...] + total_b[...]) / norm_ref[...]
    scale = jnp.broadcast_to(scale, (128, scale.shape[1])).T
    shrink = scale[:, :1] * weight_ref[...].astype(F32)
    out_ref[...] = (grad + shrink).astype(BF16)


def grad_decoder(code_t, errors, terms, weight, block=512):
    latents, features = weight.shape
    tokens = code_t.shape[1]
    rows, width = errors[0].shape
    return pl.pallas_call(
        grad_dec_kernel,
        out_shape=(
            jax.ShapeDtypeStruct((latents, features), BF16),
            jax.ShapeDtypeStruct((8, EXTRA), F32),
        ),
        grid=(latents // block,),
        in_specs=[pl.BlockSpec((block, tokens), lambda i: (i, 0))]
        + [whole((rows, width))] * 4
        + [pl.BlockSpec((1, block), lambda i: (0, i))] * 3
        + [pl.BlockSpec((block, features), lambda i: (i, 0))],
        out_specs=(
            pl.BlockSpec((block, features), lambda i: (i, 0)),
            whole((8, EXTRA)),
        ),
        scratch_shapes=[pltpu.VMEM((tokens, features), BF16)],
        cost_estimate=cost(2 * tokens * features * latents, code_t, *errors, weight, weight),
        compiler_params=params(),
    )(code_t, *errors, *terms, weight)


def grad_enc_kernel(token_ref, pre_grad_ref, out_ref):
    out_ref[...] = jnp.dot(
        token_ref[...], pre_grad_ref[...], preferred_element_type=F32
    ).astype(BF16)


def grad_encoder(token_t, pre_grad, block=1024):
    features, tokens = token_t.shape
    latents = pre_grad.shape[1]
    return pl.pallas_call(
        grad_enc_kernel,
        out_shape=jax.ShapeDtypeStruct((features, latents), BF16),
        grid=(features // block,),
        in_specs=[pl.BlockSpec((block, tokens), lambda i: (i, 0)), whole(pre_grad.shape)],
        out_specs=pl.BlockSpec((block, latents), lambda i: (i, 0)),
        cost_estimate=cost(2 * tokens * features * latents, token_t, token_t, pre_grad),
        compiler_params=params(),
    )(token_t, pre_grad)


def per_device(activations, enc_weight, enc_bias, dec_weight, dec_bias, active_mask):
    rows = activations[0]
    encoder = enc_weight[0]
    decoder = dec_weight[0]
    own, features = rows.shape
    tokens, latents = active_mask.shape
    members = CHIPS // 4
    quarter = members * own
    bias = enc_bias[None]

    place = [lax.axis_index(name) for name in LATENT]
    rows, place = lax.optimization_barrier((rows, place))
    q0 = class_exchange(jnp.broadcast_to(rows[None], (members, own, features)))
    q0 = q0.reshape(quarter, features)
    q0, active_mask, decoder, place = lax.optimization_barrier(
        (q0, active_mask, decoder, place)
    )
    q123 = from_neighbours(q0)
    pre0 = jnp.dot(q0, encoder, preferred_element_type=F32)
    other0 = swap_layers(pre0.astype(BF16)).astype(F32)
    gate = ordered_gate(active_mask, place)
    dec_float = decoder.astype(F32)
    row_norm = jnp.sqrt(jnp.sum(dec_float * dec_float, axis=1) + 1e-06)
    q123, pre0, gate, row_norm = lax.optimization_barrier((q123, pre0, gate, row_norm))
    pre123 = jnp.dot(jnp.concatenate(q123), encoder, preferred_element_type=F32)
    other123 = swap_layers(pre123.astype(BF16)).astype(F32)

    latent_code = (pre123 + other123 + bias) * gate[quarter:].astype(F32)
    total123 = jnp.sum(latent_code, axis=0, keepdims=True)
    code123 = latent_code.astype(BF16)
    parts = jnp.dot(code123, decoder, preferred_element_type=F32).astype(BF16)
    received = to_neighbours(parts.reshape(3, quarter, features))
    latent_code = (pre0 + other0 + bias) * gate[:quarter].astype(F32)
    total0 = jnp.sum(latent_code, axis=0, keepdims=True)
    code0 = latent_code.astype(BF16)
    part0 = jnp.dot(code0, decoder, preferred_element_type=F32)
    code_t = transposed([code0, code123])
    received, part0, code_t = lax.optimization_barrier((received, part0, code_t))
    partial = add_quarters(part0, received)
    parts = class_exchange(partial.reshape(members, own, features))
    sent = error_blocks(parts, rows, dec_bias, total0, total123, row_norm[None])

    e0 = class_exchange(sent).reshape(quarter, features + EXTRA)
    e0, all_tokens = lax.optimization_barrier((e0, [q0, *q123]))
    e123 = from_neighbours(e0)
    token_t = transposed(all_tokens)
    norm = row_norm[None]
    grad0 = code_gradient(e0[:, :features], norm, decoder)
    grad_other0 = swap_layers(grad0.astype(BF16)).astype(F32)
    e123, grad0, grad_other0, token_t = lax.optimization_barrier(
        (e123, grad0, grad_other0, token_t)
    )
    grad123 = code_gradient(jnp.concatenate([x[:, :features] for x in e123]), norm, decoder)
    grad_other123 = swap_layers(grad123.astype(BF16)).astype(F32)
    grad_dec, loss = grad_decoder(code_t, [e0, *e123], (total0, total123, norm), decoder)
    other_loss = swap_layers(loss)
    pre_grad0 = ((grad0 + grad_other0) * gate[:quarter].astype(F32)).astype(BF16)
    pre_grad123 = ((grad123 + grad_other123) * gate[quarter:].astype(F32)).astype(BF16)
    pre_grad = jnp.concatenate([pre_grad0, pre_grad123])
    grad_enc = grad_encoder(token_t, pre_grad)
    grad_enc, loss, other_loss = lax.optimization_barrier((grad_enc, loss, other_loss))
    loss = (loss + other_loss)[0, 0]
    return (grad_enc[None], grad_dec[None], loss / (tokens * features))


def solution(mesh):
    torus = Mesh(
        mesh.devices.reshape(mesh.shape["layer"], SIDE, SIDE, SIDE),
        ("layer", *LATENT),
    )
    placed = (
        P("layer", LATENT, None),
        P("layer", None, LATENT),
        P(LATENT),
        P("layer", LATENT, None),
        P("layer", None),
        P(None, LATENT),
    )
    return jax.shard_map(
        per_device,
        mesh=torus,
        in_specs=placed,
        out_specs=(P("layer", None, LATENT), P("layer", LATENT, None), P()),
        check_vma=False,
    )
```

```python
import jax
import jax.numpy as jnp
from jax import lax
from jax.experimental import pallas as pl
from jax.experimental.pallas import tpu as pltpu
from jax.sharding import Mesh
from jax.sharding import PartitionSpec as P

LATENT = ("latent_0", "latent_1", "latent_2")
EVERY = ("layer", *LATENT)
SIDE = 4
CHIPS = SIDE**3
SPARSITY = 0.4
EXTRA = 128
MIB = 1 << 20
F32 = jnp.float32
BF16 = jnp.bfloat16

STEPS = (
    ((0, 0, 1), (-1, 0, 0), (0, 0, -1)),
    ((0, 1, 0), (1, 0, 0), (0, -1, 0)),
)


def class_groups():
    groups = [[] for _ in range(SIDE)]
    for chip in range(CHIPS):
        l0, l1, l2 = chip // 16, chip // 4 % 4, chip % 4
        groups[(l1 + 2 * l0 + l2) % SIDE].append(chip)
    return groups


def moved(quarter, sign):
    pairs = []
    for layer, steps in enumerate(STEPS):
        for chip in range(CHIPS):
            place = chip // 16, chip // 4 % 4, chip % 4
            target = [(p + sign * d) % SIDE for p, d in zip(place, steps[quarter - 1])]
            target = target[0] * 16 + target[1] * 4 + target[2]
            pairs.append((layer * CHIPS + chip, layer * CHIPS + target))
    return pairs


def class_exchange(x):
    return lax.all_to_all(x, LATENT, 0, 0, axis_index_groups=class_groups(), tiled=True)


def from_neighbours(x):
    return [lax.ppermute(x, EVERY, moved(r, -1)) for r in (1, 2, 3)]


def to_neighbours(parts):
    return [lax.ppermute(x, EVERY, moved(r, 1)) for r, x in zip((1, 2, 3), parts)]


def swap_layers(x):
    return lax.ppermute(x, "layer", [(0, 1), (1, 0)])


def params(mib=16):
    return pltpu.CompilerParams(vmem_limit_bytes=mib * MIB)


def cost(flops, *arrays):
    size = sum(a.size * a.dtype.itemsize for a in arrays)
    return pl.CostEstimate(flops=flops, bytes_accessed=size, transcendentals=0)


def whole(shape):
    return pl.BlockSpec(shape, lambda *_: (0,) * len(shape))


def gate_kernel(order_ref, mask_ref, gate_ref):
    own = 8
    blocks = gate_ref.shape[0] // own
    first = pl.program_id(0) * blocks
    for i in range(0, blocks, 2):
        pair = [
            mask_ref[pl.ds(pl.multiple_of(order_ref[first + j] * own, own), own), :]
            for j in (i, i + 1)
        ]
        gate_ref[i * own : (i + 2) * own, :] = jnp.concatenate(pair).astype(F32).astype(BF16)


def ordered_gate(mask, place):
    tokens, latents = mask.shape
    l0, l1, l2 = place
    index = jnp.arange(CHIPS, dtype=jnp.int32)
    column = index % 16
    row_class = l1 + 2 * l0 + l2 + index // 16
    order = 4 * column + (row_class - column % 4 - 2 * (column // 4) + 12) % 4
    return pl.pallas_call(
        gate_kernel,
        out_shape=jax.ShapeDtypeStruct((tokens, latents), BF16),
        grid_spec=pltpu.PrefetchScalarGridSpec(
            num_scalar_prefetch=1,
            grid=(4,),
            in_specs=[pl.BlockSpec((tokens, latents), lambda i, order_ref: (0, 0))],
            out_specs=pl.BlockSpec((tokens // 4, latents), lambda i, order_ref: (i, 0)),
        ),
        cost_estimate=cost(0, mask),
        compiler_params=params(),
    )(order.astype(jnp.int32), mask)


def add_kernel(own_ref, a_ref, b_ref, c_ref, out_ref):
    total = own_ref[...] + a_ref[...].astype(F32) + b_ref[...].astype(F32) + c_ref[...].astype(F32)
    out_ref[...] = total.astype(out_ref.dtype)


def add_quarters(own, others, block=64):
    rows, features = own.shape
    spec = pl.BlockSpec((block, features), lambda i: (i, 0))
    return pl.pallas_call(
        add_kernel,
        out_shape=jax.ShapeDtypeStruct((rows, features), BF16),
        grid=(rows // block,),
        in_specs=[spec] * 4,
        out_specs=spec,
        cost_estimate=cost(0, own, *others),
        compiler_params=params(),
    )(own, *others)


def error_kernel(parts_ref, rows_ref, bias_ref, code_a_ref, code_b_ref, norm_ref, out_ref):
    count, own, features = parts_ref.shape
    total = parts_ref[0].astype(F32)
    for i in range(1, count):
        total = total + parts_ref[i].astype(F32)
    error = total + bias_ref[...] - rows_ref[...].astype(F32)
    sparse = (code_a_ref[...] + code_b_ref[...]) * norm_ref[...]
    square = jnp.sum(jnp.sum(error * error, axis=0, keepdims=True), axis=1, keepdims=True)
    loss = 0.5 * square + SPARSITY * jnp.sum(sparse, axis=1, keepdims=True)
    loss = jnp.broadcast_to(loss, (own, EXTRA))
    high = loss.astype(BF16).astype(F32)
    middle = (loss - high).astype(BF16).astype(F32)
    low = loss - high - middle
    lane = lax.broadcasted_iota(jnp.int32, (own, EXTRA), 1)
    row = lax.broadcasted_iota(jnp.int32, (own, EXTRA), 0)
    terms = jnp.where(lane == 0, high, jnp.where(lane == 1, middle, jnp.where(lane == 2, low, 0.0)))
    terms = jnp.where(row == 0, terms, 0.0)
    sent = error.astype(BF16)
    terms = terms.astype(BF16)
    for i in range(count):
        out_ref[i, :, :features] = sent
        out_ref[i, :, features:] = terms


def error_blocks(parts, rows, bias, code_a, code_b, norm):
    count, own, features = parts.shape
    return pl.pallas_call(
        error_kernel,
        out_shape=jax.ShapeDtypeStruct((count, own, features + EXTRA), BF16),
        cost_estimate=cost(0, parts, parts),
        compiler_params=params(),
    )(parts, rows, bias, code_a, code_b, norm)


def code_gradient(error, norm, weight):
    grad = jnp.einsum("td,fd->tf", error, weight, preferred_element_type=F32)
    return grad + SPARSITY * norm


def transpose_kernel(*refs):
    parts, out_ref = refs[:-1], refs[-1]
    start = 0
    for ref in parts:
        rows = ref.shape[0]
        out_ref[:, start : start + rows] = ref[...].T
        start += rows


def transposed(parts, block=512):
    width = parts[0].shape[1]
    total = sum(x.shape[0] for x in parts)
    return pl.pallas_call(
        transpose_kernel,
        out_shape=jax.ShapeDtypeStruct((width, total), BF16),
        grid=(width // block,),
        in_specs=[pl.BlockSpec((x.shape[0], block), lambda i: (0, i)) for x in parts],
        out_specs=pl.BlockSpec((block, total), lambda i: (i, 0)),
        cost_estimate=cost(0, *parts, *parts),
        compiler_params=params(),
    )(*parts)


def grad_dec_kernel(
    code_ref, e0, e1, e2, e3, total_a, total_b, norm_ref, weight_ref, out_ref, loss_ref, joined
):
    rows = e0.shape[0]
    features = weight_ref.shape[1]

    @pl.when(pl.program_id(0) == 0)
    def _():
        loss = jnp.zeros((rows, EXTRA), F32)
        for i, ref in enumerate((e0, e1, e2, e3)):
            joined[i * rows : (i + 1) * rows, :] = ref[:, :features]
            loss = loss + ref[:, features:].astype(F32)
        loss = jnp.sum(jnp.sum(loss, axis=0, keepdims=True), axis=1, keepdims=True)
        loss_ref[...] = jnp.broadcast_to(loss, loss_ref.shape)

    grad = jnp.dot(code_ref[...], joined[...], preferred_element_type=F32)
    scale = SPARSITY * (total_a[...] + total_b[...]) / norm_ref[...]
    scale = jnp.broadcast_to(scale, (128, scale.shape[1])).T
    shrink = scale[:, :1] * weight_ref[...].astype(F32)
    out_ref[...] = (grad + shrink).astype(BF16)


def grad_decoder(code_t, errors, terms, weight, block=512):
    latents, features = weight.shape
    tokens = code_t.shape[1]
    rows, width = errors[0].shape
    return pl.pallas_call(
        grad_dec_kernel,
        out_shape=(
            jax.ShapeDtypeStruct((latents, features), BF16),
            jax.ShapeDtypeStruct((8, EXTRA), F32),
        ),
        grid=(latents // block,),
        in_specs=[pl.BlockSpec((block, tokens), lambda i: (i, 0))]
        + [whole((rows, width))] * 4
        + [pl.BlockSpec((1, block), lambda i: (0, i))] * 3
        + [pl.BlockSpec((block, features), lambda i: (i, 0))],
        out_specs=(
            pl.BlockSpec((block, features), lambda i: (i, 0)),
            whole((8, EXTRA)),
        ),
        scratch_shapes=[pltpu.VMEM((tokens, features), BF16)],
        cost_estimate=cost(2 * tokens * features * latents, code_t, *errors, weight, weight),
        compiler_params=params(),
    )(code_t, *errors, *terms, weight)


def grad_enc_kernel(token_ref, pre_grad_ref, out_ref):
    out_ref[...] = jnp.dot(
        token_ref[...], pre_grad_ref[...], preferred_element_type=F32
    ).astype(BF16)


def grad_encoder(token_t, pre_grad, block=1024):
    features, tokens = token_t.shape
    latents = pre_grad.shape[1]
    return pl.pallas_call(
        grad_enc_kernel,
        out_shape=jax.ShapeDtypeStruct((features, latents), BF16),
        grid=(features // block,),
        in_specs=[pl.BlockSpec((block, tokens), lambda i: (i, 0)), whole(pre_grad.shape)],
        out_specs=pl.BlockSpec((block, latents), lambda i: (i, 0)),
        cost_estimate=cost(2 * tokens * features * latents, token_t, token_t, pre_grad),
        compiler_params=params(),
    )(token_t, pre_grad)


def per_device(activations, enc_weight, enc_bias, dec_weight, dec_bias, active_mask):
    rows = activations[0]
    encoder = enc_weight[0]
    decoder = dec_weight[0]
    own, features = rows.shape
    tokens, latents = active_mask.shape
    members = CHIPS // 4
    quarter = members * own
    bias = enc_bias[None]

    place = [lax.axis_index(name) for name in LATENT]
    rows, place = lax.optimization_barrier((rows, place))
    q0 = class_exchange(jnp.broadcast_to(rows[None], (members, own, features)))
    q0 = q0.reshape(quarter, features)
    q0, active_mask, decoder, place = lax.optimization_barrier(
        (q0, active_mask, decoder, place)
    )
    q123 = from_neighbours(q0)
    pre0 = jnp.dot(q0, encoder, preferred_element_type=F32)
    other0 = swap_layers(pre0)
    gate = ordered_gate(active_mask, place)
    dec_float = decoder.astype(F32)
    row_norm = jnp.sqrt(jnp.sum(dec_float * dec_float, axis=1) + 1e-06)
    q123, pre0, gate, row_norm = lax.optimization_barrier((q123, pre0, gate, row_norm))
    pre123 = jnp.dot(jnp.concatenate(q123), encoder, preferred_element_type=F32)
    other123 = swap_layers(pre123.astype(BF16)).astype(F32)

    latent_code = (pre123 + other123 + bias) * gate[quarter:].astype(F32)
    total123 = jnp.sum(latent_code, axis=0, keepdims=True)
    code123 = latent_code.astype(BF16)
    parts = jnp.dot(code123, decoder, preferred_element_type=F32).astype(BF16)
    received = to_neighbours(parts.reshape(3, quarter, features))
    latent_code = (pre0 + other0 + bias) * gate[:quarter].astype(F32)
    total0 = jnp.sum(latent_code, axis=0, keepdims=True)
    code0 = latent_code.astype(BF16)
    part0 = jnp.dot(code0, decoder, preferred_element_type=F32)
    code_t = transposed([code0, code123])
    received, part0, code_t = lax.optimization_barrier((received, part0, code_t))
    partial = add_quarters(part0, received)
    parts = class_exchange(partial.reshape(members, own, features))
    sent = error_blocks(parts, rows, dec_bias, total0, total123, row_norm[None])

    e0 = class_exchange(sent).reshape(quarter, features + EXTRA)
    e0, all_tokens = lax.optimization_barrier((e0, [q0, *q123]))
    e123 = from_neighbours(e0)
    token_t = transposed(all_tokens)
    norm = row_norm[None]
    grad0 = code_gradient(e0[:, :features], norm, decoder)
    grad_other0 = swap_layers(grad0)
    e123, grad0, grad_other0, token_t = lax.optimization_barrier(
        (e123, grad0, grad_other0, token_t)
    )
    grad123 = code_gradient(jnp.concatenate([x[:, :features] for x in e123]), norm, decoder)
    grad_other123 = swap_layers(grad123.astype(BF16)).astype(F32)
    grad_dec, loss = grad_decoder(code_t, [e0, *e123], (total0, total123, norm), decoder)
    other_loss = swap_layers(loss)
    pre_grad0 = ((grad0 + grad_other0) * gate[:quarter].astype(F32)).astype(BF16)
    pre_grad123 = ((grad123 + grad_other123) * gate[quarter:].astype(F32)).astype(BF16)
    pre_grad = jnp.concatenate([pre_grad0, pre_grad123])
    grad_enc = grad_encoder(token_t, pre_grad)
    grad_enc, loss, other_loss = lax.optimization_barrier((grad_enc, loss, other_loss))
    loss = jnp.max(loss + other_loss)
    return (grad_enc[None], grad_dec[None], loss / (tokens * features))


def solution(mesh):
    torus = Mesh(
        mesh.devices.reshape(mesh.shape["layer"], SIDE, SIDE, SIDE),
        ("layer", *LATENT),
    )
    placed = (
        P("layer", LATENT, None),
        P("layer", None, LATENT),
        P(LATENT),
        P("layer", LATENT, None),
        P("layer", None),
        P(None, LATENT),
    )
    return jax.shard_map(
        per_device,
        mesh=torus,
        in_specs=placed,
        out_specs=(P("layer", None, LATENT), P("layer", LATENT, None), P()),
        check_vma=False,
    )
```
